256 devices in a mesh: tok: 32 (over y, z), voc: 8 (over x, core).
Axes of the slice: x: 4, y: 4, z: 8, core: 2. Of those that a mesh axis runs over, the one named last changes fastest.
Arguments:
- teacher_rows: bfloat16 [8192, 2048], P('tok', 'voc')
- drafter_rows: bfloat16 [8192, 2048], P('tok', 'voc')
- head: bfloat16 [2048, 16384], P(None, 'voc'), may hold values from -1 to 1
- fr_ids: int32 [16384], P('voc'), may hold values from 0 to 151935, as said below
- targets: int32 [8192], P('tok'), may hold values from 0 to 151935
- dest_index: int32 [8192], P('tok'), may hold values from -1 to 8191, as said below
- counts: int32 [32], replicated, may hold values from 64 to 256, as said below
Outputs:
- row_loss: float32 [8192], P('tok')
- drafter_grad: bfloat16 [8192, 2048], P('tok', 'voc')
The draws below stay inside these ranges and needn't reach their ends.
Inputs may be any that keep to these rules, and one draw needn't show every extreme that they name: `dest_index`: the prefill rows that name a slot name distinct slots. With blocks of 256 rows and 32 blocks, a row of prefill block b names a slot of drafter block (b + k) mod 32 for k in 0, 1, 16, 17; at most 64 rows go from one prefill block to one drafter block, and every drafter block receives exactly 64 from its own prefill block. The slots named in drafter block j are exactly its first counts[j] slots, grouped by k in that order. counts[j] is the number of prefill rows that name a slot of block j; some block is full. `fr_ids`: distinct ids.
All inputs are finite; a program needn't handle non-finite values.
Results may differ from the reference program's by a relative error of at most 0.0041.
Values may be sent and summed in bfloat16 or wider, within the bound.
A program may use at most 64 MiB of HBM per device.

```python
import math
import jax
import jax.numpy as jnp
from jax import lax

D = 2048
VOCAB = 151936
V = 16384
REACH = 4
ROWS_TOK = 256
ROWS = 8192
N_TOK = 32


def head_matrix(key):
    column_scale = jnp.exp(jax.random.uniform(jax.random.fold_in(key, 1), (V,), jnp.float32, math.log(0.3), math.log(3.0)))
    values = jax.random.normal(jax.random.fold_in(key, 2), (D, V), jnp.float32) * 0.05 * column_scale[None, :]
    return values.astype(jnp.bfloat16).astype(jnp.float32)


def id_list(key):
    return jax.random.permutation(jax.random.fold_in(key, 3), VOCAB)[:V].astype(jnp.int32)


def draw_head(key, part):
    return head_matrix(key).astype(jnp.bfloat16)


def draw_fr_ids(key, part):
    return id_list(key)


def draw_targets(key, part):
    listed = id_list(key)
    coin = jax.random.randint(jax.random.fold_in(key, 4), (ROWS,), 0, 10)
    chosen = jax.random.randint(jax.random.fold_in(key, 5), (ROWS,), 0, V)
    other = jax.random.randint(jax.random.fold_in(key, 6), (ROWS,), 0, VOCAB)
    return jnp.where(coin < 7, listed[chosen], other).astype(jnp.int32)


def hidden_rows(key, salt):
    inner = jax.random.fold_in(key, salt)
    row_scale = jnp.exp(jax.random.uniform(jax.random.fold_in(inner, 1), (ROWS, 1), jnp.float32, math.log(0.4), math.log(4.0)))
    base = jnp.clip(jax.random.normal(jax.random.fold_in(inner, 3), (ROWS, D), jnp.float32), -6.0, 6.0)
    rows = base * row_scale
    return rows.astype(jnp.bfloat16)


def draw_teacher_rows(key, part):
    return hidden_rows(key, 40)


def draw_drafter_rows(key, part):
    return hidden_rows(key, 41)


def packing(key):
    inner = jax.random.fold_in(key, 20)
    capacity = ROWS_TOK // REACH
    blocks = jnp.arange(N_TOK)
    reach_ids = jnp.arange(REACH)
    shifts = jnp.array([0, 1, N_TOK // 2, N_TOK // 2 + 1], jnp.int32)
    loads = jax.random.randint(jax.random.fold_in(inner, 1), (N_TOK, REACH), 1, capacity + 1)
    loads = loads.at[:, 0].set(capacity)
    full_block = jax.random.randint(jax.random.fold_in(inner, 2), (), 0, N_TOK)
    loads = jnp.where(blocks[:, None] == full_block, capacity, loads).astype(jnp.int32)
    counts = jnp.sum(loads, axis=1).astype(jnp.int32)
    offsets = jnp.cumsum(loads, axis=1) - loads
    keys = jax.random.split(jax.random.fold_in(inner, 3), N_TOK)

    def one_source(source, sub_key):
        receiver = (source + shifts) % N_TOK
        sends = loads[receiver, reach_ids]
        upper = jnp.cumsum(sends)
        lower = upper - sends
        order = jnp.arange(ROWS_TOK)
        which = jnp.sum((order[:, None] >= upper[None, :]).astype(jnp.int32), axis=1)
        capped = jnp.minimum(which, REACH - 1)
        within = order - lower[capped]
        dest_block = receiver[capped]
        place = offsets[dest_block, capped] + within
        values = jnp.where(which < REACH, dest_block * ROWS_TOK + place, -1)
        shuffle = jax.random.permutation(sub_key, ROWS_TOK)
        return values[jnp.argsort(shuffle)]
    dest = jax.vmap(one_source)(blocks, keys).reshape(ROWS).astype(jnp.int32)
    return (counts, dest)


def draw_counts(key, part):
    return packing(key)[0]


def draw_dest_index(key, part):
    return packing(key)[1]


def setup_inputs(seed: int = 0) -> dict:
    key_of = jax.random.split(jax.random.key(seed), 8)
    return {
        "teacher_rows": draw_teacher_rows(jax.random.fold_in(key_of[7], 71), 0),
        "drafter_rows": draw_drafter_rows(jax.random.fold_in(key_of[7], 71), 0),
        "head": draw_head(jax.random.fold_in(key_of[7], 71), 0),
        "fr_ids": draw_fr_ids(jax.random.fold_in(key_of[7], 71), 0),
        "targets": draw_targets(jax.random.fold_in(key_of[7], 71), 0),
        "dest_index": draw_dest_index(jax.random.fold_in(key_of[7], 71), 0),
        "counts": draw_counts(jax.random.fold_in(key_of[7], 71), 0),
    }


loss_scale = 16.0


def block_terms(operands, head, fr_ids):
    teach, draft, wanted, valid = operands
    teach_logit = jnp.dot(teach, head, preferred_element_type=jnp.float32)
    draft_logit = jnp.dot(draft, head, preferred_element_type=jnp.float32)
    teach_max = jnp.max(teach_logit, axis=1, keepdims=True)
    draft_max = jnp.max(draft_logit, axis=1, keepdims=True)
    teach_exp = jnp.exp(teach_logit - teach_max)
    draft_exp = jnp.exp(draft_logit - draft_max)
    teach_total = jnp.sum(teach_exp, axis=1)
    draft_total = jnp.sum(draft_exp, axis=1)
    cross = jnp.sum(teach_exp * (teach_logit - draft_logit), axis=1)
    hit_table = (wanted[:, None] == fr_ids[None, :]).astype(jnp.float32)
    hits = jnp.sum(hit_table, axis=1)
    target_logit = jnp.sum(hit_table * draft_logit, axis=1)
    teach_lse = teach_max[:, 0] + jnp.log(teach_total)
    draft_lse = draft_max[:, 0] + jnp.log(draft_total)
    row_loss = valid * (cross / teach_total - teach_lse + draft_lse + hits * (draft_lse - target_logit))
    teach_prob = teach_exp / teach_total[:, None]
    draft_prob = draft_exp / draft_total[:, None]
    grad_logit = (valid[:, None] * ((1.0 + hits)[:, None] * draft_prob - teach_prob - hit_table)).astype(jnp.bfloat16)
    summed = jnp.dot(grad_logit, head.T, preferred_element_type=jnp.float32)
    return row_loss, (loss_scale * summed).astype(jnp.bfloat16)


def reference(teacher_rows, drafter_rows, head, fr_ids, targets, dest_index, counts):
    spot = jnp.where(dest_index >= 0, dest_index, ROWS).astype(jnp.int32)
    moved = jnp.zeros((ROWS + 1, D), jnp.bfloat16).at[spot].set(teacher_rows)[:ROWS]
    places = jnp.arange(ROWS, dtype=jnp.int32)
    owner = (places // ROWS_TOK).astype(jnp.int32)
    valid = ((places % ROWS_TOK) < counts[owner]).astype(jnp.float32)
    block = 512 if ROWS % 512 == 0 else ROWS
    many = ROWS // block
    operands = (moved.reshape(many, block, D), drafter_rows.reshape(many, block, D),
                targets.reshape(many, block), valid.reshape(many, block))
    row_loss, drafter_grad = lax.map(lambda ops: block_terms(ops, head, fr_ids), operands)
    return row_loss.reshape(ROWS), drafter_grad.reshape(ROWS, D)
```

```python
import functools

import jax
import jax.numpy as jnp
from jax import lax
from jax.experimental import pallas as pl
from jax.experimental.pallas import tpu as pltpu
from jax.sharding import PartitionSpec as P

loss_scale = 16.0
MESH = pl.DeviceIdType.MESH
NT = (((1,), (1,)), ((), ()))
F32 = jnp.float32
BF16 = jnp.bfloat16


def kernel(
    n_tok,
    teach,
    draft,
    head,
    fr,
    targ,
    dest,
    counts,
    loss,
    grad,
    head_v,
    head_t,
    rows_d,
    rows_t,
    teach_v,
    pack,
    got,
    tl,
    dl,
    ed,
    hit,
    g,
    part,
    sibp,
    two,
    far_l,
    far_r,
    near,
    in_l,
    in_r,
    stats,
    load_sem,
    ag_send,
    ag_recv,
    pk_send,
    pk_recv,
    st_send,
    st_recv,
    rs_send,
    rs_recv,
):
    n, r = hit.shape
    f = teach.shape[1]
    quarter = r // 4
    half = r // 2
    fh = f // 2
    shifts = (0, 1, n_tok // 2, n_tok // 2 + 1)
    t = lax.axis_index("tok")
    v = lax.axis_index("voc")
    x = lax.div(v, 2)
    c = lax.rem(v, 2)
    xr = lax.rem(x + 1, 4)
    xl = lax.rem(x + 3, 4)
    xo = lax.rem(x + 2, 4)
    sib = x * 2 + 1 - c
    right = xr * 2 + c
    left = xl * 2 + c
    opp = xo * 2 + c
    right_s = xr * 2 + 1 - c
    left_s = xl * 2 + 1 - c
    opp_s = xo * 2 + 1 - c

    barrier = pltpu.get_barrier_semaphore()
    greet = sorted({s % n_tok for k in shifts[1:] for s in (k, n_tok - k)})
    for k in greet:
        pl.semaphore_signal(
            barrier, inc=1, device_id={"tok": lax.rem(t + k, n_tok)}, device_id_type=MESH
        )
    for i in range(1, 8):
        pl.semaphore_signal(
            barrier, inc=1, device_id={"voc": lax.rem(v + i, 8)}, device_id_type=MESH
        )

    load_d = pltpu.make_async_copy(draft, rows_d.at[v], load_sem.at[0])
    load_t = pltpu.make_async_copy(teach, teach_v, load_sem.at[1])
    load_h = [
        pltpu.make_async_copy(
            head.at[pl.ds(i * 2 * f, 2 * f)], head_v.at[i], load_sem.at[2 + i]
        )
        for i in range(4)
    ]
    load_d.start()
    load_t.start()
    for cp in load_h:
        cp.start()

    def remote(src, dst, ssem, rsem, to):
        return pltpu.make_async_remote_copy(
            src_ref=src, dst_ref=dst, send_sem=ssem, recv_sem=rsem,
            device_id=to, device_id_type=MESH,
        )

    lo, hi = pl.ds(0, half), pl.ds(half, half)

    def gather(q, rows):
        def whole(i, p, to):
            return remote(
                rows.at[p], rows.at[p], ag_send.at[q, i], ag_recv.at[q, i], {"voc": to}
            )

        def halves(i, p, h, to):
            return remote(
                rows.at[p, h], rows.at[p, h], ag_send.at[q, i], ag_recv.at[q, i], {"voc": to}
            )

        send = [
            whole(0, v, sib),
            halves(1, v, lo, right),
            halves(2, v, hi, right),
            halves(3, v, hi, left),
            halves(4, v, lo, left),
            halves(5, left, lo, right),
            halves(6, right, hi, left),
            whole(7, left, sib),
            whole(8, right, sib),
            halves(9, opp, lo, sib),
            halves(10, opp, hi, sib),
        ]
        recv = [
            whole(0, sib, sib),
            halves(1, left, lo, right),
            halves(2, left, hi, right),
            halves(3, right, hi, left),
            halves(4, right, lo, left),
            halves(5, opp, lo, right),
            halves(6, opp, hi, left),
            whole(7, left_s, sib),
            whole(8, right_s, sib),
            halves(9, opp_s, lo, sib),
            halves(10, opp_s, hi, sib),
        ]
        return send, recv

    d_send, d_recv = gather(0, rows_d)
    t_send, t_recv = gather(1, rows_t)

    load_d.wait()
    pl.semaphore_wait(barrier, len(greet) + 7)
    for i in (1, 3, 2, 4, 0):
        d_send[i].start()

    load_t.wait()
    dest_row = dest[...]
    place = lax.rem(dest_row + r, quarter)
    spot = lax.broadcasted_iota(jnp.int32, (quarter, r), 0)
    picks = []
    sizes = []
    for k in shifts:
        rel = dest_row - lax.rem(t + k, n_tok) * r
        inside = (rel >= 0) & (rel < r)
        picks.append(jnp.where(jnp.where(inside, place, -1) == spot, 1.0, 0.0).astype(F32))
        sizes.append(jnp.sum(jnp.where(inside, 1.0, 0.0).astype(F32), axis=1, keepdims=True))
    picked = jnp.dot(
        jnp.concatenate(picks, axis=0).astype(BF16), teach_v[...], preferred_element_type=F32
    ).astype(BF16)
    for i in range(4):
        pack[i, 0:quarter, :] = picked[i * quarter : (i + 1) * quarter, :]
        pack[i, quarter : quarter + 16, :] = jnp.broadcast_to(sizes[i], (16, f)).astype(BF16)
    repack = [
        remote(
            pack.at[i], got.at[i], pk_send.at[i], pk_recv.at[i],
            {"tok": lax.rem(t + shifts[i], n_tok)},
        )
        for i in range(1, 4)
    ]
    for cp in repack:
        cp.start()

    targets = targ[...].astype(F32)
    hits_sum = jnp.zeros((8, r), F32)
    for j in range(n // 128):
        ids = fr[0:1, j * 128 : (j + 1) * 128].astype(F32)
        ids = jnp.broadcast_to(ids, (128, 128)).T
        ids = jnp.concatenate([ids] * (r // 128), axis=1) if r >= 128 else ids[:, :r]
        h = jnp.where(ids == targets, 1.0, 0.0).astype(F32)
        hit[j * 128 : (j + 1) * 128, :] = h
        hits_sum = hits_sum + jnp.sum(h.reshape(16, 8, r), axis=0)
    local_hits = jnp.sum(hits_sum, axis=0, keepdims=True)

    def turn(i):
        load_h[i].wait()
        for b in range(2):
            for j in range(n // 256):
                head_t[2 * i + b, j * 256 : (j + 1) * 256, :] = head_v[
                    i, b * f : (b + 1) * f, j * 256 : (j + 1) * 256
                ].T

    turn(0)
    for cp in repack:
        cp.wait_recv()
    one = [got[i, quarter : quarter + 1, :].astype(F32) for i in range(1, 4)]
    start = [jnp.full((1, f), float(quarter), F32)]
    for i in range(2):
        start.append(start[-1] + one[i])
    rows_t[v, 0:quarter, :] = pack[0, 0:quarter, :]
    for q in range(1, 4):
        slot = lax.broadcasted_iota(jnp.int32, (quarter, f), 0).astype(F32) + float(q * quarter)
        total = jnp.zeros((quarter, f), F32)
        for i in range(3):
            mine = (slot >= start[i]) & (slot < start[i] + one[i])
            total = total + jnp.where(mine, got[i + 1, 0:quarter, :].astype(F32), 0.0)
        rows_t[v, q * quarter : (q + 1) * quarter, :] = total.astype(BF16)
    for i in (1, 3, 2, 4, 0):
        t_send[i].start()

    turn(1)
    d_recv[1].wait_recv()
    d_send[5].start()
    d_recv[3].wait_recv()
    d_send[6].start()
    turn(2)
    d_recv[2].wait_recv()
    d_send[7].start()
    d_recv[4].wait_recv()
    d_send[8].start()
    turn(3)

    tb = min(n, 512)

    def multiply(acc, rows, ks, first):
        def body(j, carry):
            sl = pl.ds(pl.multiple_of(j * tb, tb), tb)
            s = None
            for k in ks:
                d = lax.dot_general(head_t[k, sl, :], rows[k], NT, preferred_element_type=F32)
                s = d if s is None else s + d
            if not first:
                s = s + acc[sl, :]
            acc[sl, :] = s
            return carry

        lax.fori_loop(0, n // tb, body, 0)

    sb = min(n, 256)

    def fold(a, op):
        return op(a.reshape(sb // 8, 8, r), axis=0)

    def row_max(acc):
        def body(j, m):
            sl = pl.ds(pl.multiple_of(j * sb, sb), sb)
            return jnp.maximum(m, fold(acc[sl, :], jnp.max))

        m = lax.fori_loop(0, n // sb, body, jnp.full((8, r), -jnp.inf, F32))
        return jnp.max(m, axis=0, keepdims=True)

    d_recv[0].wait_recv()
    multiply(dl, rows_d, (v, sib), True)
    multiply(dl, rows_d, (left, right), False)
    d_recv[5].wait_recv()
    d_send[9].start()
    d_recv[6].wait_recv()
    d_send[10].start()
    t_recv[1].wait_recv()
    t_send[5].start()
    t_recv[3].wait_recv()
    t_send[6].start()
    d_recv[7].wait_recv()
    d_recv[8].wait_recv()
    multiply(dl, rows_d, (left_s, right_s), False)
    t_recv[2].wait_recv()
    t_send[7].start()
    t_recv[4].wait_recv()
    t_send[8].start()
    d_recv[9].wait_recv()
    d_recv[10].wait_recv()
    multiply(dl, rows_d, (opp, opp_s), False)

    draft_max = row_max(dl)

    def draft_body(j, carry):
        total, wanted = carry
        sl = pl.ds(pl.multiple_of(j * sb, sb), sb)
        d = dl[sl, :]
        e = jnp.exp(d - draft_max)
        ed[sl, :] = e
        return total + fold(e, jnp.sum), wanted + fold(hit[sl, :] * d, jnp.sum)

    zero = jnp.zeros((8, r), F32)
    draft_total, wanted = lax.fori_loop(0, n // sb, draft_body, (zero, zero))

    t_recv[0].wait_recv()
    multiply(tl, rows_t, (v, sib), True)
    multiply(tl, rows_t, (left, right), False)
    t_recv[5].wait_recv()
    t_send[9].start()
    t_recv[6].wait_recv()
    t_send[10].start()
    t_recv[7].wait_recv()
    t_recv[8].wait_recv()
    multiply(tl, rows_t, (left_s, right_s), False)
    t_recv[9].wait_recv()
    t_recv[10].wait_recv()
    multiply(tl, rows_t, (opp, opp_s), False)

    teach_max = row_max(tl)

    def teach_body(j, carry):
        total, cross = carry
        sl = pl.ds(pl.multiple_of(j * sb, sb), sb)
        a = tl[sl, :]
        e = jnp.exp(a - teach_max)
        gap = a - dl[sl, :]
        tl[sl, :] = e
        return total + fold(e, jnp.sum), cross + fold(e * gap, jnp.sum)

    teach_total, cross = lax.fori_loop(0, n // sb, teach_body, (zero, zero))

    def down(a):
        return jnp.sum(a, axis=0, keepdims=True)

    for i, row in enumerate(
        (
            teach_max,
            draft_max,
            down(teach_total),
            down(draft_total),
            down(cross),
            down(wanted),
            local_hits,
            jnp.zeros((1, r), F32),
        )
    ):
        stats[v, i : i + 1, :] = row
    st_out = [
        remote(
            stats.at[v], stats.at[v], st_send.at[i - 1], st_recv.at[i - 1],
            {"voc": lax.rem(v + i, 8)},
        )
        for i in range(1, 8)
    ]
    for cp in st_out:
        cp.start()
    for i in range(1, 8):
        p = lax.rem(v + 8 - i, 8)
        remote(
            stats.at[p], stats.at[p], st_send.at[i - 1], st_recv.at[i - 1], {"voc": p}
        ).wait_recv()

    everyone = [stats[i] for i in range(8)]

    def gathered(i):
        return jnp.concatenate([s[i : i + 1, :] for s in everyone], axis=0)

    t_maxes, d_maxes = gathered(0), gathered(1)
    t_max = jnp.max(t_maxes, axis=0, keepdims=True)
    d_max = jnp.max(d_maxes, axis=0, keepdims=True)
    t_scale = jnp.exp(t_maxes - t_max)
    d_scale = jnp.exp(d_maxes - d_max)
    t_total = down(gathered(2) * t_scale)
    d_total = down(gathered(3) * d_scale)
    cross_all = down(gathered(4) * t_scale)
    target_logit = down(gathered(5))
    hits = down(gathered(6))
    slots = lax.broadcasted_iota(jnp.int32, (1, r), 1)
    valid = jnp.where(slots < counts[t], 1.0, 0.0).astype(F32)
    t_lse = t_max + jnp.log(t_total)
    d_lse = d_max + jnp.log(d_total)
    loss[...] = valid * (
        cross_all / t_total - t_lse + d_lse + hits * (d_lse - target_logit)
    )
    d_factor = valid * (1.0 + hits) * jnp.exp(draft_max - d_max) / d_total
    t_factor = valid * jnp.exp(teach_max - t_max) / t_total

    def grad_body(j, carry):
        sl = pl.ds(pl.multiple_of(j * sb, sb), sb)
        g[sl, :] = (d_factor * ed[sl, :] - t_factor * tl[sl, :] - valid * hit[sl, :]).astype(BF16)
        return carry

    lax.fori_loop(0, n // sb, grad_body, 0)

    def back(o, to):
        for b in range(2):
            part[o, b] = jnp.dot(
                head_v[to, b * f : (b + 1) * f, :], g[...], preferred_element_type=F32
            )

    def swap(o):
        return remote(
            part.at[o, 1 - c], sibp.at[o], rs_send.at[o], rs_recv.at[o], {"voc": sib}
        )

    swaps = [swap(o) for o in range(4)]

    def near_sum(o):
        swaps[o].wait_recv()
        return part[o, c] + sibp[o]

    flo, fhi = pl.ds(0, fh), pl.ds(fh, fh)
    out_two_r = remote(two.at[flo], far_l, rs_send.at[4], rs_recv.at[4], {"voc": right})
    out_two_l = remote(two.at[fhi], far_r, rs_send.at[5], rs_recv.at[5], {"voc": left})
    out_r = [
        remote(near.at[0, s], in_l.at[s], rs_send.at[6 + i], rs_recv.at[6 + i], {"voc": right})
        for i, s in enumerate((flo, fhi))
    ]
    out_l = [
        remote(near.at[1, s], in_r.at[s], rs_send.at[8 + i], rs_recv.at[8 + i], {"voc": left})
        for i, s in enumerate((flo, fhi))
    ]

    back(2, xo)
    swaps[2].start()
    back(1, xr)
    swaps[1].start()
    two[...] = near_sum(2).astype(BF16)
    out_two_r.start()
    out_two_l.start()
    back(3, xl)
    swaps[3].start()
    swaps[1].wait_recv()
    near[0, fh:f, :] = (part[1, c, fh:f, :] + sibp[1, fh:f, :]).astype(BF16)
    out_r[1].start()
    swaps[3].wait_recv()
    near[1, 0:fh, :] = (part[3, c, 0:fh, :] + sibp[3, 0:fh, :]).astype(BF16)
    out_l[0].start()
    back(0, x)
    swaps[0].start()
    out_two_r.wait_recv()
    near[0, 0:fh, :] = (
        part[1, c, 0:fh, :] + sibp[1, 0:fh, :] + far_l[...].astype(F32)
    ).astype(BF16)
    out_r[0].start()
    out_two_l.wait_recv()
    near[1, fh:f, :] = (
        part[3, c, fh:f, :] + sibp[3, fh:f, :] + far_r[...].astype(F32)
    ).astype(BF16)
    out_l[1].start()
    mine = near_sum(0)
    for cp in out_r + out_l:
        cp.wait_recv()
    total = mine + in_l[...].astype(F32) + in_r[...].astype(F32)
    grad[...] = (loss_scale * total).T.astype(BF16)

    for cp in d_send + t_send + repack + st_out + swaps + [out_two_r, out_two_l] + out_r + out_l:
        cp.wait_send()


def per_device(n_tok, teacher_rows, drafter_rows, head, fr_ids, targets, dest_index, counts):
    r, f = teacher_rows.shape
    d, n = head.shape
    dma = pltpu.SemaphoreType.DMA
    any_spec = pl.BlockSpec(memory_space=pl.ANY)
    vmem = pl.BlockSpec(memory_space=pltpu.VMEM)
    row_loss, grad = pl.pallas_call(
        functools.partial(kernel, n_tok),
        out_shape=(
            jax.ShapeDtypeStruct((1, r), F32),
            jax.ShapeDtypeStruct((r, f), BF16),
        ),
        in_specs=[any_spec, any_spec, any_spec, vmem, vmem, vmem,
                  pl.BlockSpec(memory_space=pltpu.SMEM)],
        out_specs=(vmem, vmem),
        scratch_shapes=[
            pltpu.VMEM((4, 2 * f, n), BF16),
            pltpu.VMEM((8, n, f), BF16),
            pltpu.VMEM((8, r, f), BF16),
            pltpu.VMEM((8, r, f), BF16),
            pltpu.VMEM((r, f), BF16),
            pltpu.VMEM((4, r // 4 + 16, f), BF16),
            pltpu.VMEM((4, r // 4 + 16, f), BF16),
            pltpu.VMEM((n, r), F32),
            pltpu.VMEM((n, r), F32),
            pltpu.VMEM((n, r), F32),
            pltpu.VMEM((n, r), F32),
            pltpu.VMEM((n, r), BF16),
            pltpu.VMEM((4, 2, f, r), F32),
            pltpu.VMEM((4, f, r), F32),
            pltpu.VMEM((f, r), BF16),
            pltpu.VMEM((f // 2, r), BF16),
            pltpu.VMEM((f // 2, r), BF16),
            pltpu.VMEM((2, f, r), BF16),
            pltpu.VMEM((f, r), BF16),
            pltpu.VMEM((f, r), BF16),
            pltpu.VMEM((8, 8, r), F32),
            dma((6,)),
            dma((2, 11)),
            dma((2, 11)),
            dma((4,)),
            dma((4,)),
            dma((7,)),
            dma((7,)),
            dma((10,)),
            dma((10,)),
        ],
        compiler_params=pltpu.CompilerParams(
            collective_id=0, has_side_effects=True, vmem_limit_bytes=56 * 1024 * 1024
        ),
    )(
        teacher_rows,
        drafter_rows,
        head,
        fr_ids.reshape(1, n),
        targets.reshape(1, r),
        dest_index.reshape(1, r),
        counts,
    )
    return row_loss.reshape(r), grad


def solution(mesh):
    return jax.shard_map(
        functools.partial(per_device, mesh.shape["tok"]),
        mesh=mesh,
        in_specs=(
            P("tok", "voc"),
            P("tok", "voc"),
            P(None, "voc"),
            P("voc"),
            P("tok"),
            P("tok"),
            P(),
        ),
        out_specs=(P("tok"), P("tok", "voc")),
        check_vma=False,
    )
```

```python
import functools

import jax
import jax.numpy as jnp
from jax import lax
from jax.experimental import pallas as pl
from jax.experimental.pallas import tpu as pltpu
from jax.sharding import PartitionSpec as P

loss_scale = 16.0
MESH = pl.DeviceIdType.MESH
NT = (((1,), (1,)), ((), ()))
F32 = jnp.float32
BF16 = jnp.bfloat16


def kernel(
    n_tok,
    teach,
    draft,
    head,
    fr_hbm,
    targ_hbm,
    dest_hbm,
    counts_hbm,
    loss,
    grad,
    fr,
    targ,
    dest,
    counts,
    head_v,
    head_t,
    rows_d,
    rows_t,
    teach_v,
    pack,
    got,
    tl,
    dl,
    ed,
    hit,
    g,
    part,
    sibp,
    two,
    far,
    near,
    inn,
    stats,
    load_sem,
    ag_send,
    ag_recv,
    pk_sem,
    st_sem,
    rs_send,
    rs_recv,
):
    n, r = hit.shape
    f = teach.shape[1]
    quarter = r // 4
    half = r // 2
    fh = f // 2
    shifts = (0, 1, n_tok // 2, n_tok // 2 + 1)
    t = lax.axis_index("tok")
    v = lax.axis_index("voc")
    x = lax.div(v, 2)
    c = lax.rem(v, 2)
    xr = lax.rem(x + 1, 4)
    xl = lax.rem(x + 3, 4)
    xo = lax.rem(x + 2, 4)
    sib = x * 2 + 1 - c
    right = xr * 2 + c
    left = xl * 2 + c
    opp = xo * 2 + c
    right_s = xr * 2 + 1 - c
    left_s = xl * 2 + 1 - c
    opp_s = xo * 2 + 1 - c

    barrier = pltpu.get_barrier_semaphore()
    for k in shifts[1:]:
        pl.semaphore_signal(
            barrier, inc=1, device_id={"tok": lax.rem(t + n_tok - k, n_tok)}, device_id_type=MESH
        )
    for p in (sib, right, left):
        pl.semaphore_signal(barrier, inc=1, device_id={"voc": p}, device_id_type=MESH)

    load_d = pltpu.make_async_copy(draft, rows_d.at[v], load_sem.at[0])
    load_t = pltpu.make_async_copy(teach, teach_v, load_sem.at[1])
    load_h = [
        pltpu.make_async_copy(
            head.at[pl.ds(i * 2 * f, 2 * f)], head_v.at[i], load_sem.at[2 + i]
        )
        for i in range(4)
    ]
    load_s = [
        pltpu.make_async_copy(a, b, load_sem.at[6 + i])
        for i, (a, b) in enumerate(
            ((dest_hbm, dest), (targ_hbm, targ), (fr_hbm, fr), (counts_hbm, counts))
        )
    ]
    load_s[0].start()
    load_t.start()
    load_d.start()
    for cp in load_s[1:]:
        cp.start()

    def remote(src, dst, ssem, rsem, to):
        return pltpu.make_async_remote_copy(
            src_ref=src, dst_ref=dst, send_sem=ssem, recv_sem=rsem,
            device_id=to, device_id_type=MESH,
        )

    lo, hi = pl.ds(0, half), pl.ds(half, half)

    def gather(q, rows):
        def piece(i, p, to, h=None):
            ref = rows.at[p] if h is None else rows.at[p, h]
            return remote(ref, ref, ag_send.at[q], ag_recv.at[q, i], {"voc": to})

        send = [
            piece(0, v, sib),
            piece(1, v, right, lo),
            piece(2, v, right, hi),
            piece(1, v, left, hi),
            piece(2, v, left, lo),
            piece(3, left, right, lo),
            piece(3, right, left, hi),
            piece(4, left, sib),
            piece(4, right, sib),
            piece(5, opp, sib, lo),
            piece(5, opp, sib, hi),
        ]
        one = rows.at[v]
        pair = rows.at[pl.ds(0, 2)]
        recv = [
            remote(ref, ref, ag_send.at[q], ag_recv.at[q, i], {"voc": sib})
            for i, ref in enumerate((one, one, one, one, pair, one))
        ]
        seven = rows.at[pl.ds(0, 7)]
        return send, recv, remote(seven, seven, ag_send.at[q], ag_recv.at[q, 0], {"voc": sib})

    d_send, d_recv, d_all = gather(0, rows_d)
    t_send, t_recv, t_all = gather(1, rows_t)

    load_s[0].wait()
    load_t.wait()
    for cp in load_h:
        cp.start()
    dest_row = dest[...]
    place = lax.rem(dest_row + r, quarter)
    spot = lax.broadcasted_iota(jnp.int32, (quarter, r), 0)
    picks = []
    sizes = []
    for k in shifts:
        rel = dest_row - lax.rem(t + k, n_tok) * r
        inside = (rel >= 0) & (rel < r)
        picks.append(jnp.where(jnp.where(inside, place, -1) == spot, 1.0, 0.0).astype(F32))
        sizes.append(jnp.sum(jnp.where(inside, 1.0, 0.0).astype(F32), axis=1, keepdims=True))
    picked = jnp.dot(
        jnp.concatenate(picks, axis=0).astype(BF16), teach_v[...], preferred_element_type=F32
    ).astype(BF16)
    for i in range(4):
        pack[i, 0:quarter, :] = picked[i * quarter : (i + 1) * quarter, :]
        pack[i, quarter : quarter + 16, :] = jnp.broadcast_to(sizes[i], (16, f)).astype(BF16)
    repack = [
        remote(
            pack.at[i], got.at[i], pk_sem.at[0], pk_sem.at[1],
            {"tok": lax.rem(t + shifts[i], n_tok)},
        )
        for i in range(1, 4)
    ]
    pl.semaphore_wait(barrier, 6)
    for cp in repack:
        cp.start()
    load_d.wait()
    for i in (1, 3, 2, 4, 0):
        d_send[i].start()

    for cp in load_s[1:]:
        cp.wait()
    targets = targ[...].astype(F32)
    hits_sum = jnp.zeros((8, r), F32)
    for j in range(n // 128):
        ids = fr[0:1, j * 128 : (j + 1) * 128].astype(F32)
        ids = jnp.broadcast_to(ids, (128, 128)).T
        ids = jnp.concatenate([ids] * (r // 128), axis=1) if r >= 128 else ids[:, :r]
        h = jnp.where(ids == targets, 1.0, 0.0).astype(F32)
        hit[j * 128 : (j + 1) * 128, :] = h
        hits_sum = hits_sum + jnp.sum(h.reshape(16, 8, r), axis=0)
    local_hits = jnp.sum(hits_sum, axis=0, keepdims=True)

    def turn(i):
        load_h[i].wait()
        for b in range(2):
            for j in range(n // 256):
                head_t[2 * i + b, j * 256 : (j + 1) * 256, :] = head_v[
                    i, b * f : (b + 1) * f, j * 256 : (j + 1) * 256
                ].T

    all_packs = remote(
        pack.at[pl.ds(1, 3)], got.at[pl.ds(1, 3)], pk_sem.at[0], pk_sem.at[1], {"voc": sib}
    )
    turn(0)
    turn(1)
    d_recv[1].wait_recv()
    d_send[5].start()
    d_send[6].start()
    all_packs.wait_recv()
    one = [got[i, quarter : quarter + 1, :].astype(F32) for i in range(1, 4)]
    start = [jnp.full((1, f), float(quarter), F32)]
    for i in range(2):
        start.append(start[-1] + one[i])
    rows_t[v, 0:quarter, :] = pack[0, 0:quarter, :]
    for q in range(1, 4):
        slot = lax.broadcasted_iota(jnp.int32, (quarter, f), 0).astype(F32) + float(q * quarter)
        total = jnp.zeros((quarter, f), F32)
        for i in range(3):
            mine = (slot >= start[i]) & (slot < start[i] + one[i])
            total = total + jnp.where(mine, got[i + 1, 0:quarter, :].astype(F32), 0.0)
        rows_t[v, q * quarter : (q + 1) * quarter, :] = total.astype(BF16)
    for i in (1, 3, 2, 4, 0):
        t_send[i].start()

    d_recv[2].wait_recv()
    d_send[7].start()
    d_send[8].start()
    turn(2)
    turn(3)
    d_recv[3].wait_recv()
    d_send[9].start()
    d_send[10].start()

    def multiply(acc, rows, ks, first):
        @pl.when(v >= 0)
        def _():
            a = jnp.concatenate([head_t[k] for k in ks], axis=1)
            b = jnp.concatenate([rows[k] for k in ks], axis=1)
            s = lax.dot_general(a, b, NT, preferred_element_type=F32)
            acc[...] = s if first else acc[...] + s

    sb = min(n, 256)

    def fold(a, op):
        return op(a.reshape(sb // 8, 8, r), axis=0)

    def row_max(acc):
        def body(j, m):
            sl = pl.ds(pl.multiple_of(j * sb, sb), sb)
            return jnp.maximum(m, fold(acc[sl, :], jnp.max))

        m = lax.fori_loop(0, n // sb, body, jnp.full((8, r), -jnp.inf, F32))
        return jnp.max(m, axis=0, keepdims=True)

    d_recv[0].wait_recv()
    multiply(dl, rows_d, (v, sib, left, right), True)
    t_recv[1].wait_recv()
    t_send[5].start()
    t_send[6].start()
    d_recv[4].wait_recv()
    d_recv[5].wait_recv()
    multiply(dl, rows_d, (left_s, right_s, opp, opp_s), False)
    t_recv[2].wait_recv()
    t_send[7].start()
    t_send[8].start()
    t_recv[0].wait_recv()
    multiply(tl, rows_t, (v, sib, left, right), True)
    t_recv[3].wait_recv()
    t_send[9].start()
    t_send[10].start()
    draft_max = row_max(dl)

    def draft_body(j, carry):
        total, wanted = carry
        sl = pl.ds(pl.multiple_of(j * sb, sb), sb)
        d = dl[sl, :]
        e = jnp.exp(d - draft_max)
        ed[sl, :] = e
        return total + fold(e, jnp.sum), wanted + fold(hit[sl, :] * d, jnp.sum)

    zero = jnp.zeros((8, r), F32)
    draft_total, wanted = lax.fori_loop(0, n // sb, draft_body, (zero, zero))

    t_recv[4].wait_recv()
    multiply(tl, rows_t, (left_s, right_s), False)
    t_recv[5].wait_recv()
    multiply(tl, rows_t, (opp, opp_s), False)

    teach_max = row_max(tl)

    def teach_body(j, carry):
        total, cross = carry
        sl = pl.ds(pl.multiple_of(j * sb, sb), sb)
        a = tl[sl, :]
        e = jnp.exp(a - teach_max)
        gap = a - dl[sl, :]
        tl[sl, :] = e
        return total + fold(e, jnp.sum), cross + fold(e * gap, jnp.sum)

    teach_total, cross = lax.fori_loop(0, n // sb, teach_body, (zero, zero))

    def down(a):
        return jnp.sum(a, axis=0, keepdims=True)

    for i, row in enumerate(
        (
            teach_max,
            draft_max,
            down(teach_total),
            down(draft_total),
            down(cross),
            down(wanted),
            local_hits,
            jnp.zeros((1, r), F32),
        )
    ):
        stats[v, i : i + 1, :] = row
    st_out = [
        remote(stats.at[v], stats.at[v], st_sem.at[0], st_sem.at[1], {"voc": p})
        for p in (opp, opp_s, right, right_s, left, left_s, sib)
    ]
    for cp in st_out:
        cp.start()
    seven = stats.at[pl.ds(0, 7)]
    all_stats = remote(seven, seven, st_sem.at[0], st_sem.at[1], {"voc": sib})
    all_stats.wait_recv()

    everyone = [stats[i] for i in range(8)]

    def gathered(i):
        return jnp.concatenate([s[i : i + 1, :] for s in everyone], axis=0)

    t_maxes, d_maxes = gathered(0), gathered(1)
    t_max = jnp.max(t_maxes, axis=0, keepdims=True)
    d_max = jnp.max(d_maxes, axis=0, keepdims=True)
    t_scale = jnp.exp(t_maxes - t_max)
    d_scale = jnp.exp(d_maxes - d_max)
    t_total = down(gathered(2) * t_scale)
    d_total = down(gathered(3) * d_scale)
    cross_all = down(gathered(4) * t_scale)
    target_logit = down(gathered(5))
    hits = down(gathered(6))
    slots = lax.broadcasted_iota(jnp.int32, (1, r), 1)
    valid = jnp.where(slots < counts[t], 1.0, 0.0).astype(F32)
    t_lse = t_max + jnp.log(t_total)
    d_lse = d_max + jnp.log(d_total)
    loss[...] = valid * (
        cross_all / t_total - t_lse + d_lse + hits * (d_lse - target_logit)
    )
    d_factor = valid * (1.0 + hits) * jnp.exp(draft_max - d_max) / d_total
    t_factor = valid * jnp.exp(teach_max - t_max) / t_total

    def grad_body(j, carry):
        sl = pl.ds(pl.multiple_of(j * sb, sb), sb)
        g[sl, :] = (d_factor * ed[sl, :] - t_factor * tl[sl, :] - valid * hit[sl, :]).astype(BF16)
        return carry

    lax.fori_loop(0, n // sb, grad_body, 0)

    def back(o, to, which):
        @pl.when(v >= 0)
        def _():
            for b in which:
                rows = pl.ds(b * f, f)
                if not isinstance(b, int):
                    rows = pl.ds(pl.multiple_of(b * f, f), f)
                part[o, b] = jnp.dot(head_v[to, rows, :], g[...], preferred_element_type=F32)

    swaps = [
        remote(part.at[o, 1 - c], sibp.at[o], rs_send.at[0], rs_recv.at[o], {"voc": sib})
        for o in range(4)
    ]

    flo, fhi = pl.ds(0, fh), pl.ds(fh, fh)
    out_two_r = remote(two.at[flo], far.at[flo], rs_send.at[1], rs_recv.at[4], {"voc": right})
    out_two_l = remote(two.at[fhi], far.at[fhi], rs_send.at[1], rs_recv.at[5], {"voc": left})

    def out_near(i, h, to):
        return remote(near.at[i, h], inn.at[i, h], rs_send.at[2], rs_recv.at[6], {"voc": to})

    back(2, xo, (1 - c,))
    swaps[2].start()
    back(2, xo, (c,))
    back(1, xr, (0, 1))
    swaps[1].start()
    swaps[2].wait_recv()
    two[...] = (part[2, c] + sibp[2]).astype(BF16)
    out_two_r.start()
    out_two_l.start()
    back(3, xl, (0, 1))
    swaps[3].start()
    swaps[1].wait_recv()
    near[0, fh:f, :] = (part[1, c, fh:f, :] + sibp[1, fh:f, :]).astype(BF16)
    out_near(0, fhi, right).start()
    back(0, x, (0, 1))
    swaps[0].start()
    swaps[3].wait_recv()
    near[1, 0:fh, :] = (part[3, c, 0:fh, :] + sibp[3, 0:fh, :]).astype(BF16)
    out_near(1, flo, left).start()
    out_two_r.wait_recv()
    near[0, 0:fh, :] = (
        part[1, c, 0:fh, :] + sibp[1, 0:fh, :] + far[0:fh, :].astype(F32)
    ).astype(BF16)
    out_near(0, flo, right).start()
    out_two_l.wait_recv()
    near[1, fh:f, :] = (
        part[3, c, fh:f, :] + sibp[3, fh:f, :] + far[fh:f, :].astype(F32)
    ).astype(BF16)
    out_near(1, fhi, left).start()
    swaps[0].wait_recv()
    mine = part[0, c] + sibp[0]
    both = remote(near, inn, rs_send.at[2], rs_recv.at[6], {"voc": sib})
    both.wait_recv()
    total = mine + inn[0].astype(F32) + inn[1].astype(F32)
    grad[...] = (loss_scale * total).T.astype(BF16)

    all_swaps = remote(sibp, sibp, rs_send.at[0], rs_recv.at[0], {"voc": sib})
    all_two = remote(two, far, rs_send.at[1], rs_recv.at[4], {"voc": sib})
    for cp in (d_all, t_all, all_packs, all_stats, all_swaps, all_two, both):
        cp.wait_send()


def per_device(n_tok, teacher_rows, drafter_rows, head, fr_ids, targets, dest_index, counts):
    r, f = teacher_rows.shape
    d, n = head.shape
    dma = pltpu.SemaphoreType.DMA
    any_spec = pl.BlockSpec(memory_space=pl.ANY)
    vmem = pl.BlockSpec(memory_space=pltpu.VMEM)
    row_loss, grad = pl.pallas_call(
        functools.partial(kernel, n_tok),
        out_shape=(
            pltpu.VMEM((1, r), F32),
            pltpu.VMEM((r, f), BF16),
        ),
        in_specs=[any_spec] * 7,
        out_specs=(vmem, vmem),
        scratch_shapes=[
            pltpu.VMEM((1, n), jnp.int32),
            pltpu.VMEM((1, r), jnp.int32),
            pltpu.VMEM((1, r), jnp.int32),
            pltpu.SMEM((n_tok,), jnp.int32),
            pltpu.VMEM((4, 2 * f, n), BF16),
            pltpu.VMEM((8, n, f), BF16),
            pltpu.VMEM((8, r, f), BF16),
            pltpu.VMEM((8, r, f), BF16),
            pltpu.VMEM((r, f), BF16),
            pltpu.VMEM((4, r // 4 + 16, f), BF16),
            pltpu.VMEM((4, r // 4 + 16, f), BF16),
            pltpu.VMEM((n, r), F32),
            pltpu.VMEM((n, r), F32),
            pltpu.VMEM((n, r), F32),
            pltpu.VMEM((n, r), F32),
            pltpu.VMEM((n, r), BF16),
            pltpu.VMEM((4, 2, f, r), F32),
            pltpu.VMEM((4, f, r), F32),
            pltpu.VMEM((f, r), BF16),
            pltpu.VMEM((f, r), BF16),
            pltpu.VMEM((2, f, r), BF16),
            pltpu.VMEM((2, f, r), BF16),
            pltpu.VMEM((8, 8, r), F32),
            dma((10,)),
            dma((2,)),
            dma((2, 6)),
            dma((2,)),
            dma((2,)),
            dma((3,)),
            dma((7,)),
        ],
        compiler_params=pltpu.CompilerParams(
            collective_id=0, has_side_effects=True, vmem_limit_bytes=56 * 1024 * 1024
        ),
    )(
        teacher_rows,
        drafter_rows,
        head,
        fr_ids.reshape(1, n),
        targets.reshape(1, r),
        dest_index.reshape(1, r),
        counts,
    )
    return row_loss.reshape(r), grad


def solution(mesh):
    return jax.shard_map(
        functools.partial(per_device, mesh.shape["tok"]),
        mesh=mesh,
        in_specs=(
            P("tok", "voc"),
            P("tok", "voc"),
            P(None, "voc"),
            P("voc"),
            P("tok"),
            P("tok"),
            P(),
        ),
        out_specs=(P("tok"), P("tok", "voc")),
        check_vma=False,
    )
```

```python
import functools

import jax
import jax.numpy as jnp
from jax import lax
from jax.experimental import pallas as pl
from jax.experimental.pallas import tpu as pltpu
from jax.sharding import PartitionSpec as P

loss_scale = 16.0
MESH = pl.DeviceIdType.MESH
NT = (((1,), (1,)), ((), ()))
F32 = jnp.float32
BF16 = jnp.bfloat16


def kernel(
    n_tok,
    teach,
    draft,
    head,
    fr_hbm,
    targ_hbm,
    dest_hbm,
    counts_hbm,
    loss,
    grad,
    fr,
    targ,
    dest,
    counts,
    head_v,
    head_t,
    rows_d,
    rows_t,
    teach_v,
    pack,
    got,
    tl,
    dl,
    ed,
    hit,
    g,
    part,
    sibp,
    far_part,
    swap_two,
    two,
    far,
    near,
    inn,
    stats,
    top,
    load_sem,
    ag_send,
    ag_recv,
    ea_recv,
    pk_sem,
    st_sem,
    rs_send,
    rs_recv,
):
    n, r = hit.shape
    f = teach.shape[1]
    quarter = r // 4
    fh = f // 2
    shifts = (0, 1, n_tok // 2, n_tok // 2 + 1)
    t = lax.axis_index("tok")
    v = lax.axis_index("voc")
    x = lax.div(v, 2)
    c = lax.rem(v, 2)
    xr = lax.rem(x + 1, 4)
    xl = lax.rem(x + 3, 4)
    xo = lax.rem(x + 2, 4)
    sib = x * 2 + 1 - c
    right = xr * 2 + c
    left = xl * 2 + c
    opp = xo * 2 + c
    right_s = xr * 2 + 1 - c
    left_s = xl * 2 + 1 - c
    opp_s = xo * 2 + 1 - c

    barrier = pltpu.get_barrier_semaphore()
    for k in shifts[1:]:
        pl.semaphore_signal(
            barrier, inc=1, device_id={"tok": lax.rem(t + n_tok - k, n_tok)}, device_id_type=MESH
        )
    for p in (sib, right, left):
        pl.semaphore_signal(barrier, inc=1, device_id={"voc": p}, device_id_type=MESH)

    load_d = pltpu.make_async_copy(draft, rows_d.at[v], load_sem.at[0])
    load_t = pltpu.make_async_copy(teach, teach_v, load_sem.at[1])
    load_h = [
        pltpu.make_async_copy(
            head.at[pl.ds(i * 2 * f, 2 * f)], head_v.at[i], load_sem.at[2 + i]
        )
        for i in range(4)
    ]
    load_s = [
        pltpu.make_async_copy(a, b, load_sem.at[6 + i])
        for i, (a, b) in enumerate(
            ((dest_hbm, dest), (targ_hbm, targ), (fr_hbm, fr), (counts_hbm, counts))
        )
    ]
    load_s[0].start()
    load_t.start()
    load_d.start()
    for cp in load_s[1:] + load_h:
        cp.start()

    def remote(src, dst, ssem, rsem, to):
        return pltpu.make_async_remote_copy(
            src_ref=src, dst_ref=dst, send_sem=ssem, recv_sem=rsem,
            device_id=to, device_id_type=MESH,
        )

    def gather(q, rows, skip):
        h = (r - skip) // 2
        lo, hi = pl.ds(skip, h), pl.ds(skip + h, h)
        every = pl.ds(skip, 2 * h)

        def piece(i, p, to, h=None):
            ref = rows.at[p, every] if h is None else rows.at[p, h]
            return remote(ref, ref, ag_send.at[q], ag_recv.at[q, i], {"voc": to})

        send = [
            piece(0, v, sib),
            piece(1, v, right, lo),
            piece(2, v, right, hi),
            piece(1, v, left, hi),
            piece(2, v, left, lo),
            piece(3, left, right, lo),
            piece(3, right, left, hi),
            piece(4, left, sib),
            piece(4, right, sib),
            piece(5, opp, sib, lo),
            piece(5, opp, sib, hi),
        ]
        one = rows.at[v, every]
        pair = rows.at[pl.ds(0, 2), every]
        recv = [
            remote(ref, ref, ag_send.at[q], ag_recv.at[q, i], {"voc": sib})
            for i, ref in enumerate((one, one, one, one, pair, one))
        ]
        seven = rows.at[pl.ds(0, 7), every]
        return send, recv, remote(seven, seven, ag_send.at[q], ag_recv.at[q, 0], {"voc": sib})

    d_send, d_recv, d_all = gather(0, rows_d, 0)
    t_send, t_recv, t_all = gather(1, rows_t, quarter)

    kept = pl.ds(0, quarter)

    def early(p, to, i):
        ref = rows_t.at[p, kept]
        return remote(ref, ref, ag_send.at[2], ea_recv.at[i], {"voc": to})

    def early_wait(count, i):
        ref = rows_t.at[pl.ds(0, count), kept]
        return remote(ref, ref, ag_send.at[2], ea_recv.at[i], {"voc": sib})

    early_near = [early(v, right, 0), early(v, left, 0), early(v, sib, 1)]
    early_far = early(v, opp, 0)
    early_pass = [early(p, sib, 1) for p in (left, right, opp)]

    load_s[0].wait()
    load_t.wait()
    dest_row = dest[...]
    place = lax.rem(dest_row + r, quarter)
    spot = lax.broadcasted_iota(jnp.int32, (quarter, r), 0)
    picks = []
    sizes = []
    for k in shifts:
        rel = dest_row - lax.rem(t + k, n_tok) * r
        inside = (rel >= 0) & (rel < r)
        picks.append(jnp.where(jnp.where(inside, place, -1) == spot, 1.0, 0.0).astype(F32))
        sizes.append(jnp.sum(jnp.where(inside, 1.0, 0.0).astype(F32), axis=1, keepdims=True))
    picked = jnp.dot(
        jnp.concatenate(picks, axis=0).astype(BF16), teach_v[...], preferred_element_type=F32
    ).astype(BF16)
    for i in range(4):
        pack[i, 0:quarter, :] = picked[i * quarter : (i + 1) * quarter, :]
        pack[i, quarter : quarter + 16, :] = jnp.broadcast_to(sizes[i], (16, f)).astype(BF16)
    repack = [
        remote(
            pack.at[i], got.at[i], pk_sem.at[0], pk_sem.at[1],
            {"tok": lax.rem(t + shifts[i], n_tok)},
        )
        for i in range(1, 4)
    ]
    rows_t[v, 0:quarter, :] = pack[0, 0:quarter, :]
    pl.semaphore_wait(barrier, 6)
    for cp in repack:
        cp.start()
    load_d.wait()
    for i in (1, 3, 0):
        d_send[i].start()

    for cp in load_s[1:]:
        cp.wait()
    targets = targ[...].astype(F32)
    hits_sum = jnp.zeros((8, r), F32)
    for j in range(n // 128):
        ids = fr[0:1, j * 128 : (j + 1) * 128].astype(F32)
        ids = jnp.broadcast_to(ids, (128, 128)).T
        ids = jnp.concatenate([ids] * (r // 128), axis=1) if r >= 128 else ids[:, :r]
        h = jnp.where(ids == targets, 1.0, 0.0).astype(F32)
        hit[j * 128 : (j + 1) * 128, :] = h
        hits_sum = hits_sum + jnp.sum(h.reshape(16, 8, r), axis=0)
    local_hits = jnp.sum(hits_sum, axis=0, keepdims=True)

    def turn(i):
        load_h[i].wait()
        for b in range(2):
            for j in range(n // 256):
                head_t[2 * i + b, j * 256 : (j + 1) * 256, :] = head_v[
                    i, b * f : (b + 1) * f, j * 256 : (j + 1) * 256
                ].T

    all_packs = remote(
        pack.at[pl.ds(1, 3)], got.at[pl.ds(1, 3)], pk_sem.at[0], pk_sem.at[1], {"voc": sib}
    )
    turn(0)
    d_send[2].start()
    d_send[4].start()
    turn(1)
    turn(2)
    for cp in early_near:
        cp.start()
    d_recv[1].wait_recv()
    d_send[5].start()
    d_send[6].start()
    early_far.start()
    turn(3)
    d_recv[2].wait_recv()
    d_send[7].start()
    d_send[8].start()
    all_packs.wait_recv()
    one = [got[i, quarter : quarter + 1, :].astype(F32) for i in range(1, 4)]
    start = [jnp.full((1, f), float(quarter), F32)]
    for i in range(2):
        start.append(start[-1] + one[i])
    for q in range(1, 4):
        slot = lax.broadcasted_iota(jnp.int32, (quarter, f), 0).astype(F32) + float(q * quarter)
        total = jnp.zeros((quarter, f), F32)
        for i in range(3):
            mine = (slot >= start[i]) & (slot < start[i] + one[i])
            total = total + jnp.where(mine, got[i + 1, 0:quarter, :].astype(F32), 0.0)
        rows_t[v, q * quarter : (q + 1) * quarter, :] = total.astype(BF16)
    for i in (1, 3, 0):
        t_send[i].start()
    def multiply(acc, rows, ks, first, last=False):
        @pl.when(v >= 0)
        def _():
            a = jnp.concatenate([head_t[k] for k in ks], axis=1)
            b = jnp.concatenate([rows[k] for k in ks], axis=1)
            s = lax.dot_general(a, b, NT, preferred_element_type=F32)
            if not first:
                s = acc[...] + s
            acc[...] = s
            if last:
                top[...] = jnp.max(s.reshape(n // 8, 8, r), axis=0)

    sb = min(n, 256)

    def fold(a, op):
        return op(a.reshape(sb // 8, 8, r), axis=0)

    d_recv[0].wait_recv()
    multiply(dl, rows_d, (v, sib, left, right), True)
    t_send[2].start()
    t_send[4].start()

    @pl.when(v >= 0)
    def _():
        ones = hit[...].astype(BF16)
        far_part[2] = jnp.dot(head_v[xo], ones, preferred_element_type=F32)

    d_recv[3].wait_recv()
    d_send[9].start()
    d_send[10].start()
    early_wait(3, 0).wait_recv()
    for cp in early_pass:
        cp.start()
    d_recv[4].wait_recv()
    multiply(dl, rows_d, (left_s, right_s), False)
    t_recv[1].wait_recv()
    t_send[5].start()
    t_send[6].start()
    d_recv[5].wait_recv()
    multiply(dl, rows_d, (opp, opp_s), False, True)
    draft_max = jnp.max(top[...], axis=0, keepdims=True)

    def draft_body(j, carry):
        total, wanted = carry
        sl = pl.ds(pl.multiple_of(j * sb, sb), sb)
        d = dl[sl, :]
        e = jnp.exp(d - draft_max)
        ed[sl, :] = e
        return total + fold(e, jnp.sum), wanted + fold(hit[sl, :] * d, jnp.sum)

    zero = jnp.zeros((8, r), F32)
    draft_total, wanted = lax.fori_loop(0, n // sb, draft_body, (zero, zero))

    t_recv[2].wait_recv()
    t_send[7].start()
    t_send[8].start()
    t_recv[0].wait_recv()
    early_wait(4, 1).wait_recv()
    multiply(tl, rows_t, (v, sib, left, right), True)
    t_recv[3].wait_recv()
    t_send[9].start()
    t_send[10].start()
    t_recv[4].wait_recv()
    multiply(tl, rows_t, (left_s, right_s), False)
    t_recv[5].wait_recv()
    multiply(tl, rows_t, (opp, opp_s), False, True)

    teach_max = jnp.max(top[...], axis=0, keepdims=True)

    def teach_body(j, carry):
        total, cross = carry
        sl = pl.ds(pl.multiple_of(j * sb, sb), sb)
        a = tl[sl, :]
        e = jnp.exp(a - teach_max)
        gap = a - dl[sl, :]
        tl[sl, :] = e
        return total + fold(e, jnp.sum), cross + fold(e * gap, jnp.sum)

    teach_total, cross = lax.fori_loop(0, n // sb, teach_body, (zero, zero))

    def down(a):
        return jnp.sum(a, axis=0, keepdims=True)

    for i, row in enumerate(
        (
            teach_max,
            draft_max,
            down(teach_total),
            down(draft_total),
            down(cross),
            down(wanted),
            local_hits,
            jnp.zeros((1, r), F32),
        )
    ):
        stats[v, i : i + 1, :] = row
    st_out = [
        remote(stats.at[v], stats.at[v], st_sem.at[0], st_sem.at[1], {"voc": p})
        for p in (opp, opp_s, right, right_s, left, left_s, sib)
    ]
    for cp in st_out:
        cp.start()
    seven = stats.at[pl.ds(0, 7)]
    all_stats = remote(seven, seven, st_sem.at[0], st_sem.at[1], {"voc": sib})

    def unscaled(i, ref):
        @pl.when(v >= 0)
        def _():
            e = ref[...]
            top_bits = e.astype(BF16)
            rest = (e - top_bits.astype(F32)).astype(BF16)
            far_part[i] = jnp.dot(head_v[xo], top_bits, preferred_element_type=F32) + jnp.dot(
                head_v[xo], rest, preferred_element_type=F32
            )

    unscaled(0, ed)
    unscaled(1, tl)
    all_stats.wait_recv()

    everyone = [stats[i] for i in range(8)]

    def gathered(i):
        return jnp.concatenate([s[i : i + 1, :] for s in everyone], axis=0)

    t_maxes, d_maxes = gathered(0), gathered(1)
    t_max = jnp.max(t_maxes, axis=0, keepdims=True)
    d_max = jnp.max(d_maxes, axis=0, keepdims=True)
    t_scale = jnp.exp(t_maxes - t_max)
    d_scale = jnp.exp(d_maxes - d_max)
    t_total = down(gathered(2) * t_scale)
    d_total = down(gathered(3) * d_scale)
    cross_all = down(gathered(4) * t_scale)
    target_logit = down(gathered(5))
    hits = down(gathered(6))
    slots = lax.broadcasted_iota(jnp.int32, (1, r), 1)
    valid = jnp.where(slots < counts[t], 1.0, 0.0).astype(F32)
    t_lse = t_max + jnp.log(t_total)
    d_lse = d_max + jnp.log(d_total)
    loss[...] = valid * (
        cross_all / t_total - t_lse + d_lse + hits * (d_lse - target_logit)
    )
    d_factor = valid * (1.0 + hits) * jnp.exp(draft_max - d_max) / d_total
    t_factor = valid * jnp.exp(teach_max - t_max) / t_total

    def back(o, to, which, first=False):
        @pl.when(v >= 0)
        def _():
            rhs = g[...] if not first else (
                d_factor * ed[...] - t_factor * tl[...] - valid * hit[...]
            ).astype(BF16)
            if first:
                g[...] = rhs
            for b in which:
                rows = pl.ds(b * f, f)
                if not isinstance(b, int):
                    rows = pl.ds(pl.multiple_of(b * f, f), f)
                part[o, b] = jnp.dot(head_v[to, rows, :], rhs, preferred_element_type=F32)

    swaps = {
        o: remote(part.at[o, 1 - c], sibp.at[o], rs_send.at[0], rs_recv.at[o], {"voc": sib})
        for o in (0, 1, 3)
    }
    swap_far = remote(swap_two.at[0], swap_two.at[1], rs_send.at[3], rs_recv.at[2], {"voc": sib})

    fq = f // 4
    quads = [pl.ds(i * fq, fq) for i in range(4)]
    flo, fhi = pl.ds(0, fh), pl.ds(fh, fh)
    ways = (right, right, left, left)
    out_two = [
        remote(two.at[q], far.at[q], rs_send.at[1], rs_recv.at[4 + i], {"voc": ways[i]})
        for i, q in enumerate(quads)
    ]

    def out_near(i, h, to):
        return remote(near.at[i, h], inn.at[i, h], rs_send.at[2], rs_recv.at[8], {"voc": to})


    def far_sum(b):
        rows = pl.ds(pl.multiple_of(b * f, f), f)
        return d_factor * far_part[0, rows] - t_factor * far_part[1, rows] - valid * far_part[2, rows]

    swap_two[0] = far_sum(1 - c).astype(BF16)
    swap_far.start()
    part[2, 0] = far_sum(c)
    back(1, xr, (0, 1), True)
    swaps[1].start()
    swap_far.wait_recv()
    two[...] = (part[2, 0] + swap_two[1].astype(F32)).astype(BF16)
    for i in (0, 2, 1, 3):
        out_two[i].start()
    back(3, xl, (0, 1))
    swaps[3].start()
    swaps[1].wait_recv()
    near[0, fh:f, :] = (part[1, c, fh:f, :] + sibp[1, fh:f, :]).astype(BF16)
    out_near(0, fhi, right).start()
    back(0, x, (0, 1))
    swaps[0].start()
    swaps[3].wait_recv()
    near[1, 0:fh, :] = (part[3, c, 0:fh, :] + sibp[3, 0:fh, :]).astype(BF16)
    out_near(1, flo, left).start()
    for i in (0, 2, 1, 3):
        out_two[i].wait_recv()
        side, o = i // 2, 1 + i // 2 * 2
        a, b = i * fq, (i + 1) * fq
        near[side, a:b, :] = (
            part[o, c, a:b, :] + sibp[o, a:b, :] + far[a:b, :].astype(F32)
        ).astype(BF16)
        out_near(side, quads[i], ways[i]).start()
    swaps[0].wait_recv()
    mine = part[0, c] + sibp[0]
    both = remote(near, inn, rs_send.at[2], rs_recv.at[8], {"voc": sib})
    both.wait_recv()
    total = mine + inn[0].astype(F32) + inn[1].astype(F32)
    grad[...] = (loss_scale * total).T.astype(BF16)

    three = sibp.at[pl.ds(0, 3)]
    all_swaps = remote(three, three, rs_send.at[0], rs_recv.at[0], {"voc": sib})
    all_two = remote(two, far, rs_send.at[1], rs_recv.at[4], {"voc": sib})
    for cp in (d_all, t_all, early_wait(7, 0), swap_far, all_packs, all_stats, all_swaps, all_two, both):
        cp.wait_send()


def per_device(n_tok, teacher_rows, drafter_rows, head, fr_ids, targets, dest_index, counts):
    r, f = teacher_rows.shape
    d, n = head.shape
    dma = pltpu.SemaphoreType.DMA
    any_spec = pl.BlockSpec(memory_space=pl.ANY)
    vmem = pl.BlockSpec(memory_space=pltpu.VMEM)
    row_loss, grad = pl.pallas_call(
        functools.partial(kernel, n_tok),
        out_shape=(
            pltpu.VMEM((1, r), F32),
            pltpu.VMEM((r, f), BF16),
        ),
        in_specs=[any_spec] * 7,
        out_specs=(vmem, vmem),
        scratch_shapes=[
            pltpu.VMEM((1, n), jnp.int32),
            pltpu.VMEM((1, r), jnp.int32),
            pltpu.VMEM((1, r), jnp.int32),
            pltpu.SMEM((n_tok,), jnp.int32),
            pltpu.VMEM((4, 2 * f, n), BF16),
            pltpu.VMEM((8, n, f), BF16),
            pltpu.VMEM((8, r, f), BF16),
            pltpu.VMEM((8, r, f), BF16),
            pltpu.VMEM((r, f), BF16),
            pltpu.VMEM((4, r // 4 + 16, f), BF16),
            pltpu.VMEM((4, r // 4 + 16, f), BF16),
            pltpu.VMEM((n, r), F32),
            pltpu.VMEM((n, r), F32),
            pltpu.VMEM((n, r), F32),
            pltpu.VMEM((n, r), F32),
            pltpu.VMEM((n, r), BF16),
            pltpu.VMEM((4, 2, f, r), F32),
            pltpu.VMEM((4, f, r), F32),
            pltpu.VMEM((3, 2 * f, r), F32),
            pltpu.VMEM((2, f, r), BF16),
            pltpu.VMEM((f, r), BF16),
            pltpu.VMEM((f, r), BF16),
            pltpu.VMEM((2, f, r), BF16),
            pltpu.VMEM((2, f, r), BF16),
            pltpu.VMEM((8, 8, r), F32),
            pltpu.VMEM((8, r), F32),
            dma((10,)),
            dma((3,)),
            dma((2, 6)),
            dma((2,)),
            dma((2,)),
            dma((2,)),
            dma((4,)),
            dma((9,)),
        ],
        compiler_params=pltpu.CompilerParams(
            collective_id=0, has_side_effects=True, vmem_limit_bytes=56 * 1024 * 1024
        ),
    )(
        teacher_rows,
        drafter_rows,
        head,
        fr_ids.reshape(1, n),
        targets.reshape(1, r),
        dest_index.reshape(1, r),
        counts,
    )
    return row_loss.reshape(r), grad


def solution(mesh):
    return jax.shard_map(
        functools.partial(per_device, mesh.shape["tok"]),
        mesh=mesh,
        in_specs=(
            P("tok", "voc"),
            P("tok", "voc"),
            P(None, "voc"),
            P("voc"),
            P("tok"),
            P("tok"),
            P(),
        ),
        out_specs=(P("tok"), P("tok", "voc")),
        check_vma=False,
    )
```

```python
import functools

import jax
import jax.numpy as jnp
from jax import lax
from jax.experimental import pallas as pl
from jax.experimental.pallas import tpu as pltpu
from jax.sharding import PartitionSpec as P

loss_scale = 16.0
MESH = pl.DeviceIdType.MESH
NT = (((1,), (1,)), ((), ()))
F32 = jnp.float32
BF16 = jnp.bfloat16


def kernel(
    n_tok,
    teach,
    draft,
    head,
    fr_hbm,
    targ_hbm,
    dest_hbm,
    counts_hbm,
    loss,
    grad,
    fr,
    targ,
    dest,
    counts,
    head_v,
    head_t,
    rows_d,
    rows_t,
    teach_v,
    pack,
    got,
    tl,
    dl,
    ed,
    hit,
    g,
    part,
    sibp,
    far_part,
    swap_two,
    two,
    far,
    near,
    inn,
    stats,
    top,
    load_sem,
    ag_send,
    ag_recv,
    ea_recv,
    pk_sem,
    st_sem,
    rs_send,
    rs_recv,
):
    n, r = hit.shape
    f = teach.shape[1]
    quarter = r // 4
    fh = f // 2
    shifts = (0, 1, n_tok // 2, n_tok // 2 + 1)
    t = lax.axis_index("tok")
    v = lax.axis_index("voc")
    x = lax.div(v, 2)
    c = lax.rem(v, 2)
    xr = lax.rem(x + 1, 4)
    xl = lax.rem(x + 3, 4)
    xo = lax.rem(x + 2, 4)
    sib = x * 2 + 1 - c
    right = xr * 2 + c
    left = xl * 2 + c
    opp = xo * 2 + c
    right_s = xr * 2 + 1 - c
    left_s = xl * 2 + 1 - c
    opp_s = xo * 2 + 1 - c

    barrier = pltpu.get_barrier_semaphore()
    for k in shifts[1:]:
        pl.semaphore_signal(
            barrier, inc=1, device_id={"tok": lax.rem(t + n_tok - k, n_tok)}, device_id_type=MESH
        )
    for p in (sib, right, left):
        pl.semaphore_signal(barrier, inc=1, device_id={"voc": p}, device_id_type=MESH)

    load_d = pltpu.make_async_copy(draft, rows_d.at[v], load_sem.at[0])
    load_t = pltpu.make_async_copy(teach, teach_v, load_sem.at[1])
    load_h = [
        pltpu.make_async_copy(
            head.at[pl.ds(i * 2 * f, 2 * f)], head_v.at[i], load_sem.at[2 + i]
        )
        for i in range(4)
    ]
    load_s = [
        pltpu.make_async_copy(a, b, load_sem.at[6 + i])
        for i, (a, b) in enumerate(
            ((dest_hbm, dest), (targ_hbm, targ), (fr_hbm, fr), (counts_hbm, counts))
        )
    ]
    load_s[0].start()
    load_t.start()
    load_d.start()
    for cp in load_s[1:] + load_h:
        cp.start()

    def remote(src, dst, ssem, rsem, to):
        return pltpu.make_async_remote_copy(
            src_ref=src, dst_ref=dst, send_sem=ssem, recv_sem=rsem,
            device_id=to, device_id_type=MESH,
        )

    def gather(q, rows, skip):
        h = (r - skip) // 2
        lo, hi = pl.ds(skip, h), pl.ds(skip + h, h)
        every = pl.ds(skip, 2 * h)

        def piece(i, p, to, h=None):
            ref = rows.at[p, every] if h is None else rows.at[p, h]
            return remote(ref, ref, ag_send.at[q], ag_recv.at[q, i], {"voc": to})

        send = [
            piece(0, v, sib),
            piece(1, v, right, lo),
            piece(2, v, right, hi),
            piece(1, v, left, hi),
            piece(2, v, left, lo),
            piece(3, left, right, lo),
            piece(3, right, left, hi),
            piece(4, left, sib),
            piece(4, right, sib),
            piece(5, opp, sib, lo),
            piece(5, opp, sib, hi),
        ]
        one = rows.at[v, every]
        pair = rows.at[pl.ds(0, 2), every]
        recv = [
            remote(ref, ref, ag_send.at[q], ag_recv.at[q, i], {"voc": sib})
            for i, ref in enumerate((one, one, one, one, pair, one))
        ]
        seven = rows.at[pl.ds(0, 7), every]
        return send, recv, remote(seven, seven, ag_send.at[q], ag_recv.at[q, 0], {"voc": sib})

    d_send, d_recv, d_all = gather(0, rows_d, 0)
    t_send, t_recv, t_all = gather(1, rows_t, quarter)

    kept = pl.ds(0, quarter)

    def early(p, to, i):
        ref = rows_t.at[p, kept]
        return remote(ref, ref, ag_send.at[2], ea_recv.at[i], {"voc": to})

    def early_wait(count, i):
        ref = rows_t.at[pl.ds(0, count), kept]
        return remote(ref, ref, ag_send.at[2], ea_recv.at[i], {"voc": sib})

    early_near = [early(v, right, 0), early(v, left, 0), early(v, sib, 1)]
    early_far = early(v, opp, 0)
    early_pass = [early(p, sib, 1) for p in (left, right, opp)]

    load_s[0].wait()
    load_t.wait()
    dest_row = dest[...]
    place = lax.rem(dest_row + r, quarter)
    spot = lax.broadcasted_iota(jnp.int32, (quarter, r), 0)
    picks = []
    sizes = []
    for k in shifts:
        rel = dest_row - lax.rem(t + k, n_tok) * r
        inside = (rel >= 0) & (rel < r)
        picks.append(jnp.where(jnp.where(inside, place, -1) == spot, 1.0, 0.0).astype(F32))
        sizes.append(jnp.sum(jnp.where(inside, 1.0, 0.0).astype(F32), axis=1, keepdims=True))
    picked = jnp.dot(
        jnp.concatenate(picks, axis=0).astype(BF16), teach_v[...], preferred_element_type=F32
    ).astype(BF16)
    for i in range(4):
        pack[i, 0:quarter, :] = picked[i * quarter : (i + 1) * quarter, :]
        pack[i, quarter : quarter + 16, :] = jnp.broadcast_to(sizes[i], (16, f)).astype(BF16)
    repack = [
        remote(
            pack.at[i], got.at[i], pk_sem.at[0], pk_sem.at[1],
            {"tok": lax.rem(t + shifts[i], n_tok)},
        )
        for i in range(1, 4)
    ]
    rows_t[v, 0:quarter, :] = pack[0, 0:quarter, :]
    pl.semaphore_wait(barrier, 6)
    for cp in repack:
        cp.start()
    load_d.wait()
    for i in (1, 3, 0):
        d_send[i].start()

    for cp in load_s[1:]:
        cp.wait()
    targets = targ[...].astype(F32)
    hits_sum = jnp.zeros((8, r), F32)
    for j in range(n // 128):
        ids = fr[0:1, j * 128 : (j + 1) * 128].astype(F32)
        ids = jnp.broadcast_to(ids, (128, 128)).T
        ids = jnp.concatenate([ids] * (r // 128), axis=1) if r >= 128 else ids[:, :r]
        h = jnp.where(ids == targets, 1.0, 0.0).astype(F32)
        hit[j * 128 : (j + 1) * 128, :] = h
        hits_sum = hits_sum + jnp.sum(h.reshape(16, 8, r), axis=0)
    local_hits = jnp.sum(hits_sum, axis=0, keepdims=True)

    def turn(i):
        load_h[i].wait()
        for b in range(2):
            for j in range(n // 256):
                head_t[2 * i + b, j * 256 : (j + 1) * 256, :] = head_v[
                    i, b * f : (b + 1) * f, j * 256 : (j + 1) * 256
                ].T

    all_packs = remote(
        pack.at[pl.ds(1, 3)], got.at[pl.ds(1, 3)], pk_sem.at[0], pk_sem.at[1], {"voc": sib}
    )
    turn(0)
    d_send[2].start()
    d_send[4].start()
    turn(1)
    turn(2)
    for cp in early_near:
        cp.start()
    d_recv[1].wait_recv()
    d_send[5].start()
    d_send[6].start()
    early_far.start()
    turn(3)
    d_recv[2].wait_recv()
    d_send[7].start()
    d_send[8].start()
    all_packs.wait_recv()
    one = [got[i, quarter : quarter + 1, :].astype(F32) for i in range(1, 4)]
    start = [jnp.full((1, f), float(quarter), F32)]
    for i in range(2):
        start.append(start[-1] + one[i])
    for q in range(1, 4):
        slot = lax.broadcasted_iota(jnp.int32, (quarter, f), 0).astype(F32) + float(q * quarter)
        total = jnp.zeros((quarter, f), F32)
        for i in range(3):
            mine = (slot >= start[i]) & (slot < start[i] + one[i])
            total = total + jnp.where(mine, got[i + 1, 0:quarter, :].astype(F32), 0.0)
        rows_t[v, q * quarter : (q + 1) * quarter, :] = total.astype(BF16)
    for i in (1, 3, 0):
        t_send[i].start()
    def multiply(acc, rows, ks, first, last=False):
        @pl.when(v >= 0)
        def _():
            a = jnp.concatenate([head_t[k] for k in ks], axis=1)
            b = jnp.concatenate([rows[k] for k in ks], axis=1)
            s = lax.dot_general(a, b, NT, preferred_element_type=F32)
            if not first:
                s = acc[...] + s
            acc[...] = s
            if last:
                top[...] = jnp.max(s.reshape(n // 8, 8, r), axis=0)

    sb = min(n, 256)

    def fold(a, op):
        return op(a.reshape(sb // 8, 8, r), axis=0)

    d_recv[0].wait_recv()
    multiply(dl, rows_d, (v, sib, left, right), True)
    t_send[2].start()
    t_send[4].start()
    d_recv[3].wait_recv()
    d_send[9].start()
    d_send[10].start()
    d_recv[4].wait_recv()
    multiply(dl, rows_d, (left_s, right_s), False)
    t_recv[1].wait_recv()
    t_send[5].start()
    t_send[6].start()
    early_wait(3, 0).wait_recv()
    for cp in early_pass:
        cp.start()

    @pl.when(v >= 0)
    def _():
        ones = hit[...].astype(BF16)
        far_part[2] = jnp.dot(head_v[xo], ones, preferred_element_type=F32)

    d_recv[5].wait_recv()
    multiply(dl, rows_d, (opp, opp_s), False, True)
    draft_max = jnp.max(top[...], axis=0, keepdims=True)

    def draft_body(j, carry):
        total, wanted = carry
        sl = pl.ds(pl.multiple_of(j * sb, sb), sb)
        d = dl[sl, :]
        e = jnp.exp(d - draft_max)
        ed[sl, :] = e
        return total + fold(e, jnp.sum), wanted + fold(hit[sl, :] * d, jnp.sum)

    zero = jnp.zeros((8, r), F32)
    draft_total, wanted = lax.fori_loop(0, n // sb, draft_body, (zero, zero))

    t_recv[2].wait_recv()
    t_send[7].start()
    t_send[8].start()
    t_recv[0].wait_recv()
    early_wait(4, 1).wait_recv()
    multiply(tl, rows_t, (v, sib, left, right), True)
    t_recv[3].wait_recv()
    t_send[9].start()
    t_send[10].start()
    t_recv[4].wait_recv()
    multiply(tl, rows_t, (left_s, right_s), False)
    t_recv[5].wait_recv()
    multiply(tl, rows_t, (opp, opp_s), False, True)

    teach_max = jnp.max(top[...], axis=0, keepdims=True)

    def teach_body(j, carry):
        total, cross = carry
        sl = pl.ds(pl.multiple_of(j * sb, sb), sb)
        a = tl[sl, :]
        e = jnp.exp(a - teach_max)
        gap = a - dl[sl, :]
        tl[sl, :] = e
        return total + fold(e, jnp.sum), cross + fold(e * gap, jnp.sum)

    teach_total, cross = lax.fori_loop(0, n // sb, teach_body, (zero, zero))

    def down(a):
        return jnp.sum(a, axis=0, keepdims=True)

    for i, row in enumerate(
        (
            teach_max,
            draft_max,
            down(teach_total),
            down(draft_total),
            down(cross),
            down(wanted),
            local_hits,
            jnp.zeros((1, r), F32),
        )
    ):
        stats[v, i : i + 1, :] = row
    st_out = [
        remote(stats.at[v], stats.at[v], st_sem.at[0], st_sem.at[1], {"voc": p})
        for p in (opp, opp_s, right, right_s, left, left_s, sib)
    ]
    for cp in st_out:
        cp.start()
    seven = stats.at[pl.ds(0, 7)]
    all_stats = remote(seven, seven, st_sem.at[0], st_sem.at[1], {"voc": sib})

    def unscaled(i, ref):
        @pl.when(v >= 0)
        def _():
            e = ref[...]
            top_bits = e.astype(BF16)
            rest = (e - top_bits.astype(F32)).astype(BF16)
            far_part[i] = jnp.dot(head_v[xo], top_bits, preferred_element_type=F32) + jnp.dot(
                head_v[xo], rest, preferred_element_type=F32
            )

    unscaled(0, ed)
    unscaled(1, tl)
    all_stats.wait_recv()

    everyone = [stats[i] for i in range(8)]

    def gathered(i):
        return jnp.concatenate([s[i : i + 1, :] for s in everyone], axis=0)

    t_maxes, d_maxes = gathered(0), gathered(1)
    t_max = jnp.max(t_maxes, axis=0, keepdims=True)
    d_max = jnp.max(d_maxes, axis=0, keepdims=True)
    t_scale = jnp.exp(t_maxes - t_max)
    d_scale = jnp.exp(d_maxes - d_max)
    t_total = down(gathered(2) * t_scale)
    d_total = down(gathered(3) * d_scale)
    cross_all = down(gathered(4) * t_scale)
    target_logit = down(gathered(5))
    hits = down(gathered(6))
    slots = lax.broadcasted_iota(jnp.int32, (1, r), 1)
    valid = jnp.where(slots < counts[t], 1.0, 0.0).astype(F32)
    t_lse = t_max + jnp.log(t_total)
    d_lse = d_max + jnp.log(d_total)
    loss[...] = valid * (
        cross_all / t_total - t_lse + d_lse + hits * (d_lse - target_logit)
    )
    d_factor = valid * (1.0 + hits) * jnp.exp(draft_max - d_max) / d_total
    t_factor = valid * jnp.exp(teach_max - t_max) / t_total

    def back(o, to, which, first=False):
        @pl.when(v >= 0)
        def _():
            rhs = g[...] if not first else (
                d_factor * ed[...] - t_factor * tl[...] - valid * hit[...]
            ).astype(BF16)
            if first:
                g[...] = rhs
            for b in which:
                rows = pl.ds(b * f, f)
                if not isinstance(b, int):
                    rows = pl.ds(pl.multiple_of(b * f, f), f)
                part[o, b] = jnp.dot(head_v[to, rows, :], rhs, preferred_element_type=F32)

    swaps = {
        o: remote(part.at[o, 1 - c], sibp.at[o], rs_send.at[0], rs_recv.at[o], {"voc": sib})
        for o in (0, 1, 3)
    }
    swap_far = remote(swap_two.at[0], swap_two.at[1], rs_send.at[3], rs_recv.at[2], {"voc": sib})

    fq = f // 4
    quads = [pl.ds(i * fq, fq) for i in range(4)]
    flo, fhi = pl.ds(0, fh), pl.ds(fh, fh)
    ways = (right, right, left, left)
    out_two = [
        remote(two.at[q], far.at[q], rs_send.at[1], rs_recv.at[4 + i], {"voc": ways[i]})
        for i, q in enumerate(quads)
    ]

    def out_near(i, h, to):
        return remote(near.at[i, h], inn.at[i, h], rs_send.at[2], rs_recv.at[8], {"voc": to})


    def far_sum(b):
        rows = pl.ds(pl.multiple_of(b * f, f), f)
        return d_factor * far_part[0, rows] - t_factor * far_part[1, rows] - valid * far_part[2, rows]

    swap_two[0] = far_sum(1 - c).astype(BF16)
    swap_far.start()
    part[2, 0] = far_sum(c)
    back(1, xr, (0, 1), True)
    swaps[1].start()
    swap_far.wait_recv()
    two[...] = (part[2, 0] + swap_two[1].astype(F32)).astype(BF16)
    for i in (0, 2, 1, 3):
        out_two[i].start()
    back(3, xl, (0, 1))
    swaps[3].start()
    swaps[1].wait_recv()
    near[0, fh:f, :] = (part[1, c, fh:f, :] + sibp[1, fh:f, :]).astype(BF16)
    out_near(0, fhi, right).start()
    back(0, x, (0, 1))
    swaps[0].start()
    swaps[3].wait_recv()
    near[1, 0:fh, :] = (part[3, c, 0:fh, :] + sibp[3, 0:fh, :]).astype(BF16)
    out_near(1, flo, left).start()
    for i in (0, 2, 1, 3):
        out_two[i].wait_recv()
        side, o = i // 2, 1 + i // 2 * 2
        a, b = i * fq, (i + 1) * fq
        near[side, a:b, :] = (
            part[o, c, a:b, :] + sibp[o, a:b, :] + far[a:b, :].astype(F32)
        ).astype(BF16)
        out_near(side, quads[i], ways[i]).start()
    swaps[0].wait_recv()
    mine = part[0, c] + sibp[0]
    both = remote(near, inn, rs_send.at[2], rs_recv.at[8], {"voc": sib})
    both.wait_recv()
    total = mine + inn[0].astype(F32) + inn[1].astype(F32)
    grad[...] = (loss_scale * total).T.astype(BF16)

    three = sibp.at[pl.ds(0, 3)]
    all_swaps = remote(three, three, rs_send.at[0], rs_recv.at[0], {"voc": sib})
    all_two = remote(two, far, rs_send.at[1], rs_recv.at[4], {"voc": sib})
    for cp in (d_all, t_all, early_wait(7, 0), swap_far, all_packs, all_stats, all_swaps, all_two, both):
        cp.wait_send()


def per_device(n_tok, teacher_rows, drafter_rows, head, fr_ids, targets, dest_index, counts):
    r, f = teacher_rows.shape
    d, n = head.shape
    dma = pltpu.SemaphoreType.DMA
    any_spec = pl.BlockSpec(memory_space=pl.ANY)
    vmem = pl.BlockSpec(memory_space=pltpu.VMEM)
    row_loss, grad = pl.pallas_call(
        functools.partial(kernel, n_tok),
        out_shape=(
            pltpu.VMEM((1, r), F32),
            pltpu.VMEM((r, f), BF16),
        ),
        in_specs=[any_spec] * 7,
        out_specs=(vmem, vmem),
        scratch_shapes=[
            pltpu.VMEM((1, n), jnp.int32),
            pltpu.VMEM((1, r), jnp.int32),
            pltpu.VMEM((1, r), jnp.int32),
            pltpu.SMEM((n_tok,), jnp.int32),
            pltpu.VMEM((4, 2 * f, n), BF16),
            pltpu.VMEM((8, n, f), BF16),
            pltpu.VMEM((8, r, f), BF16),
            pltpu.VMEM((8, r, f), BF16),
            pltpu.VMEM((r, f), BF16),
            pltpu.VMEM((4, r // 4 + 16, f), BF16),
            pltpu.VMEM((4, r // 4 + 16, f), BF16),
            pltpu.VMEM((n, r), F32),
            pltpu.VMEM((n, r), F32),
            pltpu.VMEM((n, r), F32),
            pltpu.VMEM((n, r), F32),
            pltpu.VMEM((n, r), BF16),
            pltpu.VMEM((4, 2, f, r), F32),
            pltpu.VMEM((4, f, r), F32),
            pltpu.VMEM((3, 2 * f, r), F32),
            pltpu.VMEM((2, f, r), BF16),
            pltpu.VMEM((f, r), BF16),
            pltpu.VMEM((f, r), BF16),
            pltpu.VMEM((2, f, r), BF16),
            pltpu.VMEM((2, f, r), BF16),
            pltpu.VMEM((8, 8, r), F32),
            pltpu.VMEM((8, r), F32),
            dma((10,)),
            dma((3,)),
            dma((2, 6)),
            dma((2,)),
            dma((2,)),
            dma((2,)),
            dma((4,)),
            dma((9,)),
        ],
        compiler_params=pltpu.CompilerParams(
            collective_id=0, has_side_effects=True, vmem_limit_bytes=56 * 1024 * 1024
        ),
    )(
        teacher_rows,
        drafter_rows,
        head,
        fr_ids.reshape(1, n),
        targets.reshape(1, r),
        dest_index.reshape(1, r),
        counts,
    )
    return row_loss.reshape(r), grad


def solution(mesh):
    return jax.shard_map(
        functools.partial(per_device, mesh.shape["tok"]),
        mesh=mesh,
        in_specs=(
            P("tok", "voc"),
            P("tok", "voc"),
            P(None, "voc"),
            P("voc"),
            P("tok"),
            P("tok"),
            P(),
        ),
        out_specs=(P("tok"), P("tok", "voc")),
        check_vma=False,
    )
```

```python
import functools

import jax
import jax.numpy as jnp
from jax import lax
from jax.experimental import pallas as pl
from jax.experimental.pallas import tpu as pltpu
from jax.sharding import PartitionSpec as P

loss_scale = 16.0
MESH = pl.DeviceIdType.MESH
NT = (((1,), (1,)), ((), ()))
F32 = jnp.float32
BF16 = jnp.bfloat16


def kernel(
    n_tok,
    teach,
    draft,
    head,
    fr_hbm,
    targ_hbm,
    dest_hbm,
    counts_hbm,
    loss,
    grad,
    fr,
    targ,
    dest,
    counts,
    head_v,
    head_t,
    rows_d,
    rows_t,
    teach_v,
    pack,
    got,
    tl,
    dl,
    ed,
    hit,
    g,
    part,
    sibp,
    far_part,
    swap_two,
    two,
    far,
    near,
    inn,
    stats,
    top,
    load_sem,
    ag_send,
    ag_recv,
    ea_recv,
    pk_sem,
    st_sem,
    rs_send,
    rs_recv,
):
    n, r = hit.shape
    f = teach.shape[1]
    quarter = r // 4
    fh = f // 2
    shifts = (0, 1, n_tok // 2, n_tok // 2 + 1)
    t = lax.axis_index("tok")
    v = lax.axis_index("voc")
    x = lax.div(v, 2)
    c = lax.rem(v, 2)
    xr = lax.rem(x + 1, 4)
    xl = lax.rem(x + 3, 4)
    xo = lax.rem(x + 2, 4)
    sib = x * 2 + 1 - c
    right = xr * 2 + c
    left = xl * 2 + c
    opp = xo * 2 + c
    right_s = xr * 2 + 1 - c
    left_s = xl * 2 + 1 - c
    opp_s = xo * 2 + 1 - c

    barrier = pltpu.get_barrier_semaphore()
    for k in shifts[1:]:
        pl.semaphore_signal(
            barrier, inc=1, device_id={"tok": lax.rem(t + n_tok - k, n_tok)}, device_id_type=MESH
        )
    for p in (sib, right, left):
        pl.semaphore_signal(barrier, inc=1, device_id={"voc": p}, device_id_type=MESH)

    load_d = pltpu.make_async_copy(draft, rows_d.at[v], load_sem.at[0])
    load_t = pltpu.make_async_copy(teach, teach_v, load_sem.at[1])
    load_h = [
        pltpu.make_async_copy(
            head.at[pl.ds(i * 2 * f, 2 * f)], head_v.at[i], load_sem.at[2 + i]
        )
        for i in range(4)
    ]
    load_s = [
        pltpu.make_async_copy(a, b, load_sem.at[6 + i])
        for i, (a, b) in enumerate(
            ((dest_hbm, dest), (targ_hbm, targ), (fr_hbm, fr), (counts_hbm, counts))
        )
    ]
    load_s[0].start()
    load_t.start()
    load_d.start()
    for cp in load_s[1:] + load_h:
        cp.start()

    def remote(src, dst, ssem, rsem, to):
        return pltpu.make_async_remote_copy(
            src_ref=src, dst_ref=dst, send_sem=ssem, recv_sem=rsem,
            device_id=to, device_id_type=MESH,
        )

    def gather(q, rows, skip):
        h = (r - skip) // 2
        lo, hi = pl.ds(skip, h), pl.ds(skip + h, h)
        every = pl.ds(skip, 2 * h)

        def piece(i, p, to, h=None):
            ref = rows.at[p, every] if h is None else rows.at[p, h]
            return remote(ref, ref, ag_send.at[q], ag_recv.at[q, i], {"voc": to})

        send = [
            piece(0, v, sib),
            piece(1, v, right, lo),
            piece(2, v, right, hi),
            piece(1, v, left, hi),
            piece(2, v, left, lo),
            piece(3, left, right, lo),
            piece(3, right, left, hi),
            piece(4, left, sib),
            piece(4, right, sib),
            piece(5, opp, sib, lo),
            piece(5, opp, sib, hi),
        ]
        one = rows.at[v, every]
        pair = rows.at[pl.ds(0, 2), every]
        recv = [
            remote(ref, ref, ag_send.at[q], ag_recv.at[q, i], {"voc": sib})
            for i, ref in enumerate((one, one, one, one, pair, one))
        ]
        seven = rows.at[pl.ds(0, 7), every]
        return send, recv, remote(seven, seven, ag_send.at[q], ag_recv.at[q, 0], {"voc": sib})

    d_send, d_recv, d_all = gather(0, rows_d, 0)
    t_send, t_recv, t_all = gather(1, rows_t, quarter)

    kept = pl.ds(0, quarter)

    def early(p, to, i):
        ref = rows_t.at[p, kept]
        return remote(ref, ref, ag_send.at[2], ea_recv.at[i], {"voc": to})

    def early_wait(count, i):
        ref = rows_t.at[pl.ds(0, count), kept]
        return remote(ref, ref, ag_send.at[2], ea_recv.at[i], {"voc": sib})

    early_near = [early(v, right, 0), early(v, left, 0), early(v, sib, 1)]
    early_far = early(v, opp, 0)
    early_pass = [early(p, sib, 1) for p in (left, right, opp)]

    load_s[0].wait()
    load_t.wait()
    dest_row = dest[...]
    place = lax.rem(dest_row + r, quarter)
    spot = lax.broadcasted_iota(jnp.int32, (quarter, r), 0)
    picks = []
    sizes = []
    for k in shifts:
        rel = dest_row - lax.rem(t + k, n_tok) * r
        inside = (rel >= 0) & (rel < r)
        picks.append(jnp.where(jnp.where(inside, place, -1) == spot, 1.0, 0.0).astype(F32))
        sizes.append(jnp.sum(jnp.where(inside, 1.0, 0.0).astype(F32), axis=1, keepdims=True))
    picked = jnp.dot(
        jnp.concatenate(picks, axis=0).astype(BF16), teach_v[...], preferred_element_type=F32
    ).astype(BF16)
    for i in range(4):
        pack[i, 0:quarter, :] = picked[i * quarter : (i + 1) * quarter, :]
        pack[i, quarter : quarter + 16, :] = jnp.broadcast_to(sizes[i], (16, f)).astype(BF16)
    repack = [
        remote(
            pack.at[i], got.at[i], pk_sem.at[0], pk_sem.at[1],
            {"tok": lax.rem(t + shifts[i], n_tok)},
        )
        for i in range(1, 4)
    ]
    rows_t[v, 0:quarter, :] = pack[0, 0:quarter, :]
    pl.semaphore_wait(barrier, 6)
    for cp in repack:
        cp.start()
    load_d.wait()
    for i in (1, 3, 0):
        d_send[i].start()

    for cp in load_s[1:]:
        cp.wait()
    targets = targ[...].astype(F32)
    hits_sum = jnp.zeros((8, r), F32)
    for j in range(n // 128):
        ids = fr[0:1, j * 128 : (j + 1) * 128].astype(F32)
        ids = jnp.broadcast_to(ids, (128, 128)).T
        ids = jnp.concatenate([ids] * (r // 128), axis=1) if r >= 128 else ids[:, :r]
        h = jnp.where(ids == targets, 1.0, 0.0).astype(F32)
        hit[j * 128 : (j + 1) * 128, :] = h
        hits_sum = hits_sum + jnp.sum(h.reshape(16, 8, r), axis=0)
    local_hits = jnp.sum(hits_sum, axis=0, keepdims=True)

    def turn(i):
        load_h[i].wait()
        for b in range(2):
            for j in range(n // 256):
                head_t[2 * i + b, j * 256 : (j + 1) * 256, :] = head_v[
                    i, b * f : (b + 1) * f, j * 256 : (j + 1) * 256
                ].T

    all_packs = remote(
        pack.at[pl.ds(1, 3)], got.at[pl.ds(1, 3)], pk_sem.at[0], pk_sem.at[1], {"voc": sib}
    )
    turn(0)
    d_send[2].start()
    d_send[4].start()
    turn(1)
    turn(2)
    for cp in early_near:
        cp.start()
    d_recv[1].wait_recv()
    d_send[5].start()
    d_send[6].start()
    early_far.start()
    turn(3)
    d_recv[2].wait_recv()
    d_send[7].start()
    d_send[8].start()
    all_packs.wait_recv()
    one = [got[i, quarter : quarter + 1, :].astype(F32) for i in range(1, 4)]
    start = [jnp.full((1, f), float(quarter), F32)]
    for i in range(2):
        start.append(start[-1] + one[i])
    for q in range(1, 4):
        slot = lax.broadcasted_iota(jnp.int32, (quarter, f), 0).astype(F32) + float(q * quarter)
        total = jnp.zeros((quarter, f), F32)
        for i in range(3):
            mine = (slot >= start[i]) & (slot < start[i] + one[i])
            total = total + jnp.where(mine, got[i + 1, 0:quarter, :].astype(F32), 0.0)
        rows_t[v, q * quarter : (q + 1) * quarter, :] = total.astype(BF16)
    for i in (1, 3, 0):
        t_send[i].start()
    def multiply(acc, rows, ks, first, last=False):
        @pl.when(v >= 0)
        def _():
            a = jnp.concatenate([head_t[k] for k in ks], axis=1)
            b = jnp.concatenate([rows[k] for k in ks], axis=1)
            s = lax.dot_general(a, b, NT, preferred_element_type=F32)
            if not first:
                s = acc[...] + s
            acc[...] = s
            if last:
                top[...] = jnp.max(s.reshape(n // 8, 8, r), axis=0)

    sb = min(n, 256)

    def fold(a, op):
        return op(a.reshape(sb // 8, 8, r), axis=0)

    d_recv[0].wait_recv()
    multiply(dl, rows_d, (v, sib, left, right), True)
    t_send[2].start()
    t_send[4].start()
    d_recv[3].wait_recv()
    d_send[9].start()
    d_send[10].start()
    d_recv[4].wait_recv()
    multiply(dl, rows_d, (left_s, right_s), False)
    t_recv[1].wait_recv()
    t_send[5].start()
    t_send[6].start()
    early_wait(3, 0).wait_recv()
    for cp in early_pass:
        cp.start()

    @pl.when(v >= 0)
    def _():
        ones = hit[...].astype(BF16)
        far_part[2] = jnp.dot(head_v[xo], ones, preferred_element_type=F32)

    d_recv[5].wait_recv()
    multiply(dl, rows_d, (opp, opp_s), False, True)
    draft_max = jnp.max(top[...], axis=0, keepdims=True)

    def draft_body(j, carry):
        total, wanted = carry
        sl = pl.ds(pl.multiple_of(j * sb, sb), sb)
        d = dl[sl, :]
        e = jnp.exp(d - draft_max)
        ed[sl, :] = e
        return total + fold(e, jnp.sum), wanted + fold(hit[sl, :] * d, jnp.sum)

    zero = jnp.zeros((8, r), F32)
    draft_total, wanted = lax.fori_loop(0, n // sb, draft_body, (zero, zero))

    t_recv[2].wait_recv()
    t_send[7].start()
    t_send[8].start()
    t_recv[0].wait_recv()
    early_wait(4, 1).wait_recv()
    multiply(tl, rows_t, (v, sib, left, right), True)
    t_recv[3].wait_recv()
    t_send[9].start()
    t_send[10].start()
    t_recv[4].wait_recv()
    multiply(tl, rows_t, (left_s, right_s), False)
    t_recv[5].wait_recv()
    multiply(tl, rows_t, (opp, opp_s), False, True)

    teach_max = jnp.max(top[...], axis=0, keepdims=True)

    def teach_body(j, carry):
        total, cross = carry
        sl = pl.ds(pl.multiple_of(j * sb, sb), sb)
        a = tl[sl, :]
        e = jnp.exp(a - teach_max)
        gap = a - dl[sl, :]
        tl[sl, :] = e
        return total + fold(e, jnp.sum), cross + fold(e * gap, jnp.sum)

    teach_total, cross = lax.fori_loop(0, n // sb, teach_body, (zero, zero))

    def down(a):
        return jnp.sum(a, axis=0, keepdims=True)

    for i, row in enumerate(
        (
            teach_max,
            draft_max,
            down(teach_total),
            down(draft_total),
            down(cross),
            down(wanted),
            local_hits,
            jnp.zeros((1, r), F32),
        )
    ):
        stats[v, i : i + 1, :] = row
    st_out = [
        remote(stats.at[v], stats.at[v], st_sem.at[0], st_sem.at[1], {"voc": p})
        for p in (opp, opp_s, right, right_s, left, left_s, sib)
    ]
    for cp in st_out:
        cp.start()
    seven = stats.at[pl.ds(0, 7)]
    all_stats = remote(seven, seven, st_sem.at[0], st_sem.at[1], {"voc": sib})

    def unscaled(i, ref):
        @pl.when(v >= 0)
        def _():
            e = ref[...]
            top_bits = e.astype(BF16)
            rest = (e - top_bits.astype(F32)).astype(BF16)
            far_part[i] = jnp.dot(head_v[xo], top_bits, preferred_element_type=F32) + jnp.dot(
                head_v[xo], rest, preferred_element_type=F32
            )

    unscaled(0, ed)
    unscaled(1, tl)
    all_stats.wait_recv()

    everyone = [stats[i] for i in range(8)]

    def gathered(i):
        return jnp.concatenate([s[i : i + 1, :] for s in everyone], axis=0)

    t_maxes, d_maxes = gathered(0), gathered(1)
    t_max = jnp.max(t_maxes, axis=0, keepdims=True)
    d_max = jnp.max(d_maxes, axis=0, keepdims=True)
    t_scale = jnp.exp(t_maxes - t_max)
    d_scale = jnp.exp(d_maxes - d_max)
    t_total = down(gathered(2) * t_scale)
    d_total = down(gathered(3) * d_scale)
    cross_all = down(gathered(4) * t_scale)
    target_logit = down(gathered(5))
    hits = down(gathered(6))
    slots = lax.broadcasted_iota(jnp.int32, (1, r), 1)
    valid = jnp.where(slots < counts[t], 1.0, 0.0).astype(F32)
    t_lse = t_max + jnp.log(t_total)
    d_lse = d_max + jnp.log(d_total)
    loss[...] = valid * (
        cross_all / t_total - t_lse + d_lse + hits * (d_lse - target_logit)
    )
    d_factor = valid * (1.0 + hits) * jnp.exp(draft_max - d_max) / d_total
    t_factor = valid * jnp.exp(teach_max - t_max) / t_total

    def back(slices, first=False):
        @pl.when(v >= 0)
        def _():
            rhs = g[...] if not first else (
                d_factor * ed[...] - t_factor * tl[...] - valid * hit[...]
            ).astype(BF16)
            if first:
                g[...] = rhs
            for o, to, a, b in slices:
                for i in range(2):
                    part[o, i, a:b] = jnp.dot(
                        head_v[to, i * f + a : i * f + b, :], rhs, preferred_element_type=F32
                    )

    def swap(o, a, b, sem):
        rows = pl.ds(a, b - a)
        return remote(
            part.at[o, 1 - c, rows], sibp.at[o, rows], rs_send.at[0], rs_recv.at[sem], {"voc": sib}
        )

    swap_r, swap_l = swap(1, fh, f, 1), swap(3, 0, fh, 3)
    swap_rest = [swap(1, 0, fh, 9), swap(3, fh, f, 9)]
    swap_own = swap(0, 0, f, 0)
    swap_far = remote(swap_two.at[0], swap_two.at[1], rs_send.at[3], rs_recv.at[2], {"voc": sib})

    fq = f // 4
    quads = [pl.ds(i * fq, fq) for i in range(4)]
    flo, fhi = pl.ds(0, fh), pl.ds(fh, fh)
    ways = (right, right, left, left)
    out_two = [
        remote(two.at[q], far.at[q], rs_send.at[1], rs_recv.at[4 + i], {"voc": ways[i]})
        for i, q in enumerate(quads)
    ]

    def out_near(i, h, to):
        return remote(near.at[i, h], inn.at[i, h], rs_send.at[2], rs_recv.at[8], {"voc": to})


    def far_sum(b):
        rows = pl.ds(pl.multiple_of(b * f, f), f)
        return d_factor * far_part[0, rows] - t_factor * far_part[1, rows] - valid * far_part[2, rows]

    swap_two[0] = far_sum(1 - c).astype(BF16)
    swap_far.start()
    part[2, 0] = far_sum(c)
    back(((1, xr, fh, f), (3, xl, 0, fh)), True)
    swap_r.start()
    swap_l.start()
    swap_far.wait_recv()
    two[...] = (part[2, 0] + swap_two[1].astype(F32)).astype(BF16)
    for i in (0, 2, 1, 3):
        out_two[i].start()
    back(((1, xr, 0, fh), (3, xl, fh, f)))
    for cp in swap_rest:
        cp.start()
    swap_r.wait_recv()
    near[0, fh:f, :] = (part[1, c, fh:f, :] + sibp[1, fh:f, :]).astype(BF16)
    out_near(0, fhi, right).start()
    swap_l.wait_recv()
    near[1, 0:fh, :] = (part[3, c, 0:fh, :] + sibp[3, 0:fh, :]).astype(BF16)
    out_near(1, flo, left).start()
    back(((0, x, 0, f),))
    swap_own.start()
    remote(sibp.at[0], sibp.at[0], rs_send.at[0], rs_recv.at[9], {"voc": sib}).wait_recv()
    for i in (0, 2, 1, 3):
        out_two[i].wait_recv()
        side, o = i // 2, 1 + i // 2 * 2
        a, b = i * fq, (i + 1) * fq
        near[side, a:b, :] = (
            part[o, c, a:b, :] + sibp[o, a:b, :] + far[a:b, :].astype(F32)
        ).astype(BF16)
        out_near(side, quads[i], ways[i]).start()
    swap_own.wait_recv()
    mine = part[0, c] + sibp[0]
    both = remote(near, inn, rs_send.at[2], rs_recv.at[8], {"voc": sib})
    both.wait_recv()
    total = mine + inn[0].astype(F32) + inn[1].astype(F32)
    grad[...] = (loss_scale * total).T.astype(BF16)

    three = sibp.at[pl.ds(0, 3)]
    all_swaps = remote(three, three, rs_send.at[0], rs_recv.at[0], {"voc": sib})
    all_two = remote(two, far, rs_send.at[1], rs_recv.at[4], {"voc": sib})
    for cp in (d_all, t_all, early_wait(7, 0), swap_far, all_packs, all_stats, all_swaps, all_two, both):
        cp.wait_send()


def per_device(n_tok, teacher_rows, drafter_rows, head, fr_ids, targets, dest_index, counts):
    r, f = teacher_rows.shape
    d, n = head.shape
    dma = pltpu.SemaphoreType.DMA
    any_spec = pl.BlockSpec(memory_space=pl.ANY)
    vmem = pl.BlockSpec(memory_space=pltpu.VMEM)
    row_loss, grad = pl.pallas_call(
        functools.partial(kernel, n_tok),
        out_shape=(
            pltpu.VMEM((1, r), F32),
            pltpu.VMEM((r, f), BF16),
        ),
        in_specs=[any_spec] * 7,
        out_specs=(vmem, vmem),
        scratch_shapes=[
            pltpu.VMEM((1, n), jnp.int32),
            pltpu.VMEM((1, r), jnp.int32),
            pltpu.VMEM((1, r), jnp.int32),
            pltpu.SMEM((n_tok,), jnp.int32),
            pltpu.VMEM((4, 2 * f, n), BF16),
            pltpu.VMEM((8, n, f), BF16),
            pltpu.VMEM((8, r, f), BF16),
            pltpu.VMEM((8, r, f), BF16),
            pltpu.VMEM((r, f), BF16),
            pltpu.VMEM((4, r // 4 + 16, f), BF16),
            pltpu.VMEM((4, r // 4 + 16, f), BF16),
            pltpu.VMEM((n, r), F32),
            pltpu.VMEM((n, r), F32),
            pltpu.VMEM((n, r), F32),
            pltpu.VMEM((n, r), F32),
            pltpu.VMEM((n, r), BF16),
            pltpu.VMEM((4, 2, f, r), F32),
            pltpu.VMEM((4, f, r), F32),
            pltpu.VMEM((3, 2 * f, r), F32),
            pltpu.VMEM((2, f, r), BF16),
            pltpu.VMEM((f, r), BF16),
            pltpu.VMEM((f, r), BF16),
            pltpu.VMEM((2, f, r), BF16),
            pltpu.VMEM((2, f, r), BF16),
            pltpu.VMEM((8, 8, r), F32),
            pltpu.VMEM((8, r), F32),
            dma((10,)),
            dma((3,)),
            dma((2, 6)),
            dma((2,)),
            dma((2,)),
            dma((2,)),
            dma((4,)),
            dma((10,)),
        ],
        compiler_params=pltpu.CompilerParams(
            collective_id=0, has_side_effects=True, vmem_limit_bytes=56 * 1024 * 1024
        ),
    )(
        teacher_rows,
        drafter_rows,
        head,
        fr_ids.reshape(1, n),
        targets.reshape(1, r),
        dest_index.reshape(1, r),
        counts,
    )
    return row_loss.reshape(r), grad


def solution(mesh):
    return jax.shard_map(
        functools.partial(per_device, mesh.shape["tok"]),
        mesh=mesh,
        in_specs=(
            P("tok", "voc"),
            P("tok", "voc"),
            P(None, "voc"),
            P("voc"),
            P("tok"),
            P("tok"),
            P(),
        ),
        out_specs=(P("tok"), P("tok", "voc")),
        check_vma=False,
    )
```

```python
import functools

import jax
import jax.numpy as jnp
from jax import lax
from jax.experimental import pallas as pl
from jax.experimental.pallas import tpu as pltpu
from jax.sharding import PartitionSpec as P

loss_scale = 16.0
MESH = pl.DeviceIdType.MESH
NT = (((1,), (1,)), ((), ()))
F32 = jnp.float32
BF16 = jnp.bfloat16


def kernel(
    n_tok,
    teach,
    draft,
    head,
    fr_hbm,
    targ_hbm,
    dest_hbm,
    counts_hbm,
    loss,
    grad,
    fr,
    targ,
    dest,
    counts,
    head_v,
    head_t,
    rows_d,
    rows_t,
    teach_v,
    pack,
    got,
    tl,
    dl,
    ed,
    hit,
    g,
    part,
    sibp,
    far_part,
    swap_two,
    two,
    far,
    near,
    inn,
    stats,
    top,
    load_sem,
    ag_send,
    ag_recv,
    ea_recv,
    pk_sem,
    st_sem,
    rs_send,
    rs_recv,
):
    n, r = hit.shape
    f = teach.shape[1]
    quarter = r // 4
    fh = f // 2
    shifts = (0, 1, n_tok // 2, n_tok // 2 + 1)
    t = lax.axis_index("tok")
    v = lax.axis_index("voc")
    x = lax.div(v, 2)
    c = lax.rem(v, 2)
    xr = lax.rem(x + 1, 4)
    xl = lax.rem(x + 3, 4)
    xo = lax.rem(x + 2, 4)
    sib = x * 2 + 1 - c
    right = xr * 2 + c
    left = xl * 2 + c
    opp = xo * 2 + c
    right_s = xr * 2 + 1 - c
    left_s = xl * 2 + 1 - c
    opp_s = xo * 2 + 1 - c

    barrier = pltpu.get_barrier_semaphore()
    for k in shifts[1:]:
        pl.semaphore_signal(
            barrier, inc=1, device_id={"tok": lax.rem(t + n_tok - k, n_tok)}, device_id_type=MESH
        )
    for p in (sib, right, left):
        pl.semaphore_signal(barrier, inc=1, device_id={"voc": p}, device_id_type=MESH)

    load_d = pltpu.make_async_copy(draft, rows_d.at[v], load_sem.at[0])
    load_t = pltpu.make_async_copy(teach, teach_v, load_sem.at[1])
    load_h = [
        pltpu.make_async_copy(
            head.at[pl.ds(i * 2 * f, 2 * f)], head_v.at[i], load_sem.at[2 + i]
        )
        for i in range(4)
    ]
    load_s = [
        pltpu.make_async_copy(a, b, load_sem.at[6 + i])
        for i, (a, b) in enumerate(
            ((dest_hbm, dest), (targ_hbm, targ), (fr_hbm, fr), (counts_hbm, counts))
        )
    ]
    load_s[0].start()
    load_t.start()
    load_d.start()
    for cp in load_s[1:] + load_h:
        cp.start()

    def remote(src, dst, ssem, rsem, to):
        return pltpu.make_async_remote_copy(
            src_ref=src, dst_ref=dst, send_sem=ssem, recv_sem=rsem,
            device_id=to, device_id_type=MESH,
        )

    def gather(q, rows, skip):
        h = (r - skip) // 2
        lo, hi = pl.ds(skip, h), pl.ds(skip + h, h)
        every = pl.ds(skip, 2 * h)

        def piece(i, p, to, h=None):
            ref = rows.at[p, every] if h is None else rows.at[p, h]
            return remote(ref, ref, ag_send.at[q], ag_recv.at[q, i], {"voc": to})

        send = [
            piece(0, v, sib),
            piece(1, v, right, lo),
            piece(2, v, right, hi),
            piece(1, v, left, hi),
            piece(2, v, left, lo),
            piece(3, left, right, lo),
            piece(3, right, left, hi),
            piece(4, left, sib),
            piece(4, right, sib),
            piece(5, opp, sib, lo),
            piece(5, opp, sib, hi),
        ]
        one = rows.at[v, every]
        pair = rows.at[pl.ds(0, 2), every]
        recv = [
            remote(ref, ref, ag_send.at[q], ag_recv.at[q, i], {"voc": sib})
            for i, ref in enumerate((one, one, one, one, pair, one))
        ]
        seven = rows.at[pl.ds(0, 7), every]
        return send, recv, remote(seven, seven, ag_send.at[q], ag_recv.at[q, 0], {"voc": sib})

    d_send, d_recv, d_all = gather(0, rows_d, 0)
    t_send, t_recv, t_all = gather(1, rows_t, quarter)

    kept = pl.ds(0, quarter)

    def early(p, to, i):
        ref = rows_t.at[p, kept]
        return remote(ref, ref, ag_send.at[2], ea_recv.at[i], {"voc": to})

    def early_wait(count, i):
        ref = rows_t.at[pl.ds(0, count), kept]
        return remote(ref, ref, ag_send.at[2], ea_recv.at[i], {"voc": sib})

    early_near = [early(v, right, 0), early(v, left, 0), early(v, sib, 1)]
    early_far = early(v, opp, 0)
    early_pass = [early(p, sib, 1) for p in (left, right, opp)]

    load_s[0].wait()
    load_t.wait()
    dest_row = dest[...]
    place = lax.rem(dest_row + r, quarter)
    spot = lax.broadcasted_iota(jnp.int32, (quarter, r), 0)
    picks = []
    sizes = []
    for k in shifts:
        rel = dest_row - lax.rem(t + k, n_tok) * r
        inside = (rel >= 0) & (rel < r)
        picks.append(jnp.where(jnp.where(inside, place, -1) == spot, 1.0, 0.0).astype(F32))
        sizes.append(jnp.sum(jnp.where(inside, 1.0, 0.0).astype(F32), axis=1, keepdims=True))
    picked = jnp.dot(
        jnp.concatenate(picks, axis=0).astype(BF16), teach_v[...], preferred_element_type=F32
    ).astype(BF16)
    for i in range(4):
        pack[i, 0:quarter, :] = picked[i * quarter : (i + 1) * quarter, :]
        pack[i, quarter : quarter + 16, :] = jnp.broadcast_to(sizes[i], (16, f)).astype(BF16)
    repack = [
        remote(
            pack.at[i], got.at[i], pk_sem.at[0], pk_sem.at[1],
            {"tok": lax.rem(t + shifts[i], n_tok)},
        )
        for i in range(1, 4)
    ]
    rows_t[v, 0:quarter, :] = pack[0, 0:quarter, :]
    pl.semaphore_wait(barrier, 6)
    for cp in repack:
        cp.start()
    load_d.wait()
    for i in (1, 3, 0):
        d_send[i].start()

    def turn(i):
        load_h[i].wait()
        for b in range(2):
            for j in range(n // 256):
                head_t[2 * i + b, j * 256 : (j + 1) * 256, :] = head_v[
                    i, b * f : (b + 1) * f, j * 256 : (j + 1) * 256
                ].T

    all_packs = remote(
        pack.at[pl.ds(1, 3)], got.at[pl.ds(1, 3)], pk_sem.at[0], pk_sem.at[1], {"voc": sib}
    )
    turn(0)
    d_send[2].start()
    d_send[4].start()
    turn(1)
    for cp in early_near:
        cp.start()
    d_recv[1].wait_recv()
    d_send[5].start()
    d_send[6].start()
    early_far.start()
    for cp in load_s[1:]:
        cp.wait()
    targets = targ[...].astype(F32)
    hits_sum = jnp.zeros((8, r), F32)
    for j in range(n // 128):
        ids = fr[0:1, j * 128 : (j + 1) * 128].astype(F32)
        ids = jnp.broadcast_to(ids, (128, 128)).T
        ids = jnp.concatenate([ids] * (r // 128), axis=1) if r >= 128 else ids[:, :r]
        h = jnp.where(ids == targets, 1.0, 0.0).astype(F32)
        hit[j * 128 : (j + 1) * 128, :] = h
        hits_sum = hits_sum + jnp.sum(h.reshape(16, 8, r), axis=0)
    local_hits = jnp.sum(hits_sum, axis=0, keepdims=True)

    turn(2)
    turn(3)
    d_recv[2].wait_recv()
    d_send[7].start()
    d_send[8].start()
    all_packs.wait_recv()
    one = [got[i, quarter : quarter + 1, :].astype(F32) for i in range(1, 4)]
    start = [jnp.full((1, f), float(quarter), F32)]
    for i in range(2):
        start.append(start[-1] + one[i])
    for q in range(1, 4):
        slot = lax.broadcasted_iota(jnp.int32, (quarter, f), 0).astype(F32) + float(q * quarter)
        total = jnp.zeros((quarter, f), F32)
        for i in range(3):
            mine = (slot >= start[i]) & (slot < start[i] + one[i])
            total = total + jnp.where(mine, got[i + 1, 0:quarter, :].astype(F32), 0.0)
        rows_t[v, q * quarter : (q + 1) * quarter, :] = total.astype(BF16)
    for i in (1, 3, 0):
        t_send[i].start()
    def multiply(acc, rows, ks, first, last=False):
        @pl.when(v >= 0)
        def _():
            a = jnp.concatenate([head_t[k] for k in ks], axis=1)
            b = jnp.concatenate([rows[k] for k in ks], axis=1)
            s = lax.dot_general(a, b, NT, preferred_element_type=F32)
            if not first:
                s = acc[...] + s
            acc[...] = s
            if last:
                top[...] = jnp.max(s.reshape(n // 8, 8, r), axis=0)

    sb = min(n, 256)

    def fold(a, op):
        return op(a.reshape(sb // 8, 8, r), axis=0)

    d_recv[0].wait_recv()
    multiply(dl, rows_d, (v, sib, left, right), True)
    t_send[2].start()
    t_send[4].start()
    d_recv[3].wait_recv()
    d_send[9].start()
    d_send[10].start()
    d_recv[4].wait_recv()
    multiply(dl, rows_d, (left_s, right_s), False)
    t_recv[1].wait_recv()
    t_send[5].start()
    t_send[6].start()
    early_wait(3, 0).wait_recv()
    for cp in early_pass:
        cp.start()

    @pl.when(v >= 0)
    def _():
        ones = hit[...].astype(BF16)
        far_part[2] = jnp.dot(head_v[xo], ones, preferred_element_type=F32)

    d_recv[5].wait_recv()
    multiply(dl, rows_d, (opp, opp_s), False, True)
    draft_max = jnp.max(top[...], axis=0, keepdims=True)

    def draft_body(j, carry):
        total, wanted = carry
        sl = pl.ds(pl.multiple_of(j * sb, sb), sb)
        d = dl[sl, :]
        e = jnp.exp(d - draft_max)
        ed[sl, :] = e
        return total + fold(e, jnp.sum), wanted + fold(hit[sl, :] * d, jnp.sum)

    zero = jnp.zeros((8, r), F32)
    draft_total, wanted = lax.fori_loop(0, n // sb, draft_body, (zero, zero))

    t_recv[2].wait_recv()
    t_send[7].start()
    t_send[8].start()
    t_recv[0].wait_recv()
    early_wait(4, 1).wait_recv()
    multiply(tl, rows_t, (v, sib, left, right), True)
    t_recv[3].wait_recv()
    t_send[9].start()
    t_send[10].start()
    t_recv[4].wait_recv()
    multiply(tl, rows_t, (left_s, right_s), False)
    t_recv[5].wait_recv()
    multiply(tl, rows_t, (opp, opp_s), False, True)

    teach_max = jnp.max(top[...], axis=0, keepdims=True)

    def teach_body(j, carry):
        total, cross = carry
        sl = pl.ds(pl.multiple_of(j * sb, sb), sb)
        a = tl[sl, :]
        e = jnp.exp(a - teach_max)
        gap = a - dl[sl, :]
        tl[sl, :] = e
        return total + fold(e, jnp.sum), cross + fold(e * gap, jnp.sum)

    teach_total, cross = lax.fori_loop(0, n // sb, teach_body, (zero, zero))

    def down(a):
        return jnp.sum(a, axis=0, keepdims=True)

    for i, row in enumerate(
        (
            teach_max,
            draft_max,
            down(teach_total),
            down(draft_total),
            down(cross),
            down(wanted),
            local_hits,
            jnp.zeros((1, r), F32),
        )
    ):
        stats[v, i : i + 1, :] = row
    st_out = [
        remote(stats.at[v], stats.at[v], st_sem.at[0], st_sem.at[1], {"voc": p})
        for p in (opp, opp_s, right, right_s, left, left_s, sib)
    ]
    for cp in st_out:
        cp.start()
    seven = stats.at[pl.ds(0, 7)]
    all_stats = remote(seven, seven, st_sem.at[0], st_sem.at[1], {"voc": sib})

    def unscaled(i, ref):
        @pl.when(v >= 0)
        def _():
            e = ref[...]
            top_bits = e.astype(BF16)
            rest = (e - top_bits.astype(F32)).astype(BF16)
            far_part[i] = jnp.dot(head_v[xo], top_bits, preferred_element_type=F32) + jnp.dot(
                head_v[xo], rest, preferred_element_type=F32
            )

    unscaled(0, ed)
    unscaled(1, tl)
    all_stats.wait_recv()

    everyone = [stats[i] for i in range(8)]

    def gathered(i):
        return jnp.concatenate([s[i : i + 1, :] for s in everyone], axis=0)

    t_maxes, d_maxes = gathered(0), gathered(1)
    t_max = jnp.max(t_maxes, axis=0, keepdims=True)
    d_max = jnp.max(d_maxes, axis=0, keepdims=True)
    t_scale = jnp.exp(t_maxes - t_max)
    d_scale = jnp.exp(d_maxes - d_max)
    t_total = down(gathered(2) * t_scale)
    d_total = down(gathered(3) * d_scale)
    cross_all = down(gathered(4) * t_scale)
    target_logit = down(gathered(5))
    hits = down(gathered(6))
    slots = lax.broadcasted_iota(jnp.int32, (1, r), 1)
    valid = jnp.where(slots < counts[t], 1.0, 0.0).astype(F32)
    t_lse = t_max + jnp.log(t_total)
    d_lse = d_max + jnp.log(d_total)
    loss[...] = valid * (
        cross_all / t_total - t_lse + d_lse + hits * (d_lse - target_logit)
    )
    d_factor = valid * (1.0 + hits) * jnp.exp(draft_max - d_max) / d_total
    t_factor = valid * jnp.exp(teach_max - t_max) / t_total

    def back(o, to, which, first=False):
        @pl.when(v >= 0)
        def _():
            rhs = g[...] if not first else (
                d_factor * ed[...] - t_factor * tl[...] - valid * hit[...]
            ).astype(BF16)
            if first:
                g[...] = rhs
            for b in which:
                rows = pl.ds(b * f, f)
                if not isinstance(b, int):
                    rows = pl.ds(pl.multiple_of(b * f, f), f)
                part[o, b] = jnp.dot(head_v[to, rows, :], rhs, preferred_element_type=F32)

    swaps = {
        o: remote(part.at[o, 1 - c], sibp.at[o], rs_send.at[0], rs_recv.at[o], {"voc": sib})
        for o in (0, 1, 3)
    }
    swap_far = remote(swap_two.at[0], swap_two.at[1], rs_send.at[3], rs_recv.at[2], {"voc": sib})

    fq = f // 4
    quads = [pl.ds(i * fq, fq) for i in range(4)]
    flo, fhi = pl.ds(0, fh), pl.ds(fh, fh)
    ways = (right, right, left, left)
    out_two = [
        remote(two.at[q], far.at[q], rs_send.at[1], rs_recv.at[4 + i], {"voc": ways[i]})
        for i, q in enumerate(quads)
    ]

    def out_near(i, h, to):
        return remote(near.at[i, h], inn.at[i, h], rs_send.at[2], rs_recv.at[8], {"voc": to})


    def far_sum(b):
        rows = pl.ds(pl.multiple_of(b * f, f), f)
        return d_factor * far_part[0, rows] - t_factor * far_part[1, rows] - valid * far_part[2, rows]

    swap_two[0] = far_sum(1 - c).astype(BF16)
    swap_far.start()
    part[2, 0] = far_sum(c)
    back(1, xr, (0, 1), True)
    swaps[1].start()
    swap_far.wait_recv()
    two[...] = (part[2, 0] + swap_two[1].astype(F32)).astype(BF16)
    for i in (0, 2, 1, 3):
        out_two[i].start()
    back(3, xl, (0, 1))
    swaps[3].start()
    swaps[1].wait_recv()
    near[0, fh:f, :] = (part[1, c, fh:f, :] + sibp[1, fh:f, :]).astype(BF16)
    out_near(0, fhi, right).start()
    back(0, x, (0, 1))
    swaps[0].start()
    swaps[3].wait_recv()
    near[1, 0:fh, :] = (part[3, c, 0:fh, :] + sibp[3, 0:fh, :]).astype(BF16)
    out_near(1, flo, left).start()
    for i in (0, 2, 1, 3):
        out_two[i].wait_recv()
        side, o = i // 2, 1 + i // 2 * 2
        a, b = i * fq, (i + 1) * fq
        near[side, a:b, :] = (
            part[o, c, a:b, :] + sibp[o, a:b, :] + far[a:b, :].astype(F32)
        ).astype(BF16)
        out_near(side, quads[i], ways[i]).start()
    swaps[0].wait_recv()
    mine = part[0, c] + sibp[0]
    both = remote(near, inn, rs_send.at[2], rs_recv.at[8], {"voc": sib})
    both.wait_recv()
    total = mine + inn[0].astype(F32) + inn[1].astype(F32)
    grad[...] = (loss_scale * total).T.astype(BF16)

    three = sibp.at[pl.ds(0, 3)]
    all_swaps = remote(three, three, rs_send.at[0], rs_recv.at[0], {"voc": sib})
    all_two = remote(two, far, rs_send.at[1], rs_recv.at[4], {"voc": sib})
    for cp in (d_all, t_all, early_wait(7, 0), swap_far, all_packs, all_stats, all_swaps, all_two, both):
        cp.wait_send()


def per_device(n_tok, teacher_rows, drafter_rows, head, fr_ids, targets, dest_index, counts):
    r, f = teacher_rows.shape
    d, n = head.shape
    dma = pltpu.SemaphoreType.DMA
    any_spec = pl.BlockSpec(memory_space=pl.ANY)
    vmem = pl.BlockSpec(memory_space=pltpu.VMEM)
    row_loss, grad = pl.pallas_call(
        functools.partial(kernel, n_tok),
        out_shape=(
            pltpu.VMEM((1, r), F32),
            pltpu.VMEM((r, f), BF16),
        ),
        in_specs=[any_spec] * 7,
        out_specs=(vmem, vmem),
        scratch_shapes=[
            pltpu.VMEM((1, n), jnp.int32),
            pltpu.VMEM((1, r), jnp.int32),
            pltpu.VMEM((1, r), jnp.int32),
            pltpu.SMEM((n_tok,), jnp.int32),
            pltpu.VMEM((4, 2 * f, n), BF16),
            pltpu.VMEM((8, n, f), BF16),
            pltpu.VMEM((8, r, f), BF16),
            pltpu.VMEM((8, r, f), BF16),
            pltpu.VMEM((r, f), BF16),
            pltpu.VMEM((4, r // 4 + 16, f), BF16),
            pltpu.VMEM((4, r // 4 + 16, f), BF16),
            pltpu.VMEM((n, r), F32),
            pltpu.VMEM((n, r), F32),
            pltpu.VMEM((n, r), F32),
            pltpu.VMEM((n, r), F32),
            pltpu.VMEM((n, r), BF16),
            pltpu.VMEM((4, 2, f, r), F32),
            pltpu.VMEM((4, f, r), F32),
            pltpu.VMEM((3, 2 * f, r), F32),
            pltpu.VMEM((2, f, r), BF16),
            pltpu.VMEM((f, r), BF16),
            pltpu.VMEM((f, r), BF16),
            pltpu.VMEM((2, f, r), BF16),
            pltpu.VMEM((2, f, r), BF16),
            pltpu.VMEM((8, 8, r), F32),
            pltpu.VMEM((8, r), F32),
            dma((10,)),
            dma((3,)),
            dma((2, 6)),
            dma((2,)),
            dma((2,)),
            dma((2,)),
            dma((4,)),
            dma((9,)),
        ],
        compiler_params=pltpu.CompilerParams(
            collective_id=0, has_side_effects=True, vmem_limit_bytes=56 * 1024 * 1024
        ),
    )(
        teacher_rows,
        drafter_rows,
        head,
        fr_ids.reshape(1, n),
        targets.reshape(1, r),
        dest_index.reshape(1, r),
        counts,
    )
    return row_loss.reshape(r), grad


def solution(mesh):
    return jax.shard_map(
        functools.partial(per_device, mesh.shape["tok"]),
        mesh=mesh,
        in_specs=(
            P("tok", "voc"),
            P("tok", "voc"),
            P(None, "voc"),
            P("voc"),
            P("tok"),
            P("tok"),
            P(),
        ),
        out_specs=(P("tok"), P("tok", "voc")),
        check_vma=False,
    )
```
